32 devices in a mesh: facet: 8 (over y, x, core), freq: 4 (over z).
Axes of the slice: x: 2, y: 2, z: 4, core: 2. Of those that a mesh axis runs over, the one named last changes fastest.
Arguments:
- residual: float32 [32, 8, 512, 512], P('freq', 'facet'), may hold values from -3 to 3
- components: bfloat16 [4, 32, 128, 128], P(None, 'freq', 'facet'), may hold values from -6 to 6
- chan_weight: float32 [32], P('freq'), may hold values from 0.3 to 3
- tile_pos: int32 [4, 2], replicated, may hold values from 0 to 1920, as said below
- facet_psf: int32 [8], P('facet'), may hold values from 0 to 3
- psf_spectra: bfloat16 [4, 32, 2, 768, 768], P(None, 'freq', None, 'facet'), may hold values from -48 to 48
Outputs:
- new_residual: float32 [32, 8, 512, 512], P('freq', 'facet')
The draws below stay inside these ranges and needn't reach their ends.
Inputs may be any that keep to these rules, and one draw needn't show every extreme that they name: `tile_pos`: each row is a tile's top-left pixel (row, column); the row never exceeds 1024 - 128 and the column never exceeds 2048 - 128; some tile lies at the image's right edge and some tile at its top edge.
All inputs are finite; a program needn't handle non-finite values.
Results may differ from the reference program's by a relative error of at most 0.0045.
Values may be sent and summed in bfloat16 or wider, within the bound.
No kernel may reach another device: no remote copies, remote signals or barrier semaphores. Data moves between devices by JAX's collectives and lax.ppermute only.
A program may use at most 256 MiB of HBM per device.

```python
import math
import jax
import jax.numpy as jnp
from jax import lax

CHAN = 32
FS = 512
PAD = 128
TS = 128
NTILE = 4
FCOLS = 4
NPSF = 4
FRAME = 768
FACETS = 8
IMG_ROWS = 1024
IMG_COLS = 2048


def draw_tile_pos(key, part):
    key_center, key_offset = jax.random.split(jax.random.fold_in(key, 11))
    center = jax.random.randint(key_center, (), 0, FACETS)
    middle_row = center // FCOLS * FS + FS // 2 - TS // 2
    middle_col = center % FCOLS * FS + FS // 2 - TS // 2
    shifts = jax.random.randint(key_offset, (NTILE, 2), -FS, FS + 1)
    tile_rows = jnp.clip(middle_row + shifts[:, 0], 0, IMG_ROWS - TS)
    tile_cols = jnp.clip(middle_col + shifts[:, 1], 0, IMG_COLS - TS)
    tile_index = jnp.arange(NTILE, dtype=jnp.int32)
    tile_cols = jnp.where(tile_index == 0, IMG_COLS - TS, tile_cols)
    tile_rows = jnp.where(tile_index == 1, 0, tile_rows)
    return jnp.stack([tile_rows, tile_cols], axis=1).astype(jnp.int32)


def touch_ends(values, stream_key, least, high):
    extent = values.shape
    place = [jax.random.randint(jax.random.fold_in(stream_key, axis), (), 0, extent[axis]) for axis in range(len(extent))]
    values = values.at[tuple(place)].set(least)
    longest = extent.index(max(extent))
    place[longest] = (place[longest] + 1) % extent[longest]
    return values.at[tuple(place)].set(high)


def block_levels(own_key, extent, cuts, smallest, top_value):
    factor_of = 1.0
    for axis_at, parts in cuts:
        draws = jax.random.uniform(jax.random.fold_in(jax.random.fold_in(own_key, 6), axis_at), (parts,), jnp.float32, smallest / len(cuts), top_value / len(cuts))
        factor_of = factor_of * jnp.repeat(jnp.exp(draws), extent[axis_at] // parts).reshape((-1,) + (1,) * (len(extent) - 1 - axis_at))
    return factor_of


def noise(stream_key, extent, width, reach, shards=(), kind=jnp.bfloat16):
    level = block_levels(stream_key, extent, shards, -0.22, 0.18) if shards else 1.0
    values = jax.random.normal(stream_key, extent, jnp.float32) * width * level
    return jnp.minimum(jnp.maximum(values, -reach), reach).astype(kind)


def setup_inputs(seed: int = 0) -> dict:
    key_of = jax.random.split(jax.random.key(seed), 7)
    residual = noise(key_of[0], (CHAN, FACETS, FS, FS), 0.5, 3.0, ((0, 4), (1, 8)), jnp.float32)
    components = noise(key_of[1], (NTILE, CHAN, TS, TS), 1.0, 6.0, ((1, 4), (2, 8)))
    chan_weight = jnp.clip(jnp.exp(math.log(3.0) - 2.3025851 * jax.random.uniform(key_of[2], (CHAN,), jnp.float32) ** block_levels(key_of[2], (CHAN,), ((0, 4),), -0.2, 0.2)), 0.3, 3.0)
    tile_pos = draw_tile_pos(jax.random.fold_in(key_of[6], 71), 0)
    facet_psf = touch_ends(jax.random.randint(key_of[4], (FACETS,), 0, NPSF), jax.random.fold_in(key_of[4], 1), 0, NPSF - 1).astype(jnp.int32)
    psf_spectra = noise(key_of[5], (NPSF, CHAN, 2, FRAME, FRAME), 8.0, 48.0, ((1, 4), (3, 8)))
    return {"residual": residual, "components": components, "chan_weight": chan_weight, "tile_pos": tile_pos, "facet_psf": facet_psf, "psf_spectra": psf_spectra}


def phase_table(positions):
    frequencies = jnp.arange(FRAME, dtype=jnp.int32)
    product = (positions[..., None] * frequencies) % FRAME
    theta = product.astype(jnp.float32) * (2.0 * math.pi / FRAME)
    return jnp.cos(theta), jnp.sin(theta)


def solve_fit(moments, gram_terms):
    g0, g1, g2, g3, g4 = gram_terms[0], gram_terms[1], gram_terms[2], gram_terms[3], gram_terms[4]
    c00 = g2 * g4 - g3 * g3
    c01 = g2 * g3 - g1 * g4
    c02 = g1 * g3 - g2 * g2
    c11 = g0 * g4 - g2 * g2
    c12 = g1 * g2 - g0 * g3
    c22 = g0 * g2 - g1 * g1
    determinant = g0 * c00 + g1 * c01 + g2 * c02
    first = (c00 * moments[0] + c01 * moments[1] + c02 * moments[2]) / determinant
    second = (c01 * moments[0] + c11 * moments[1] + c12 * moments[2]) / determinant
    third = (c02 * moments[0] + c12 * moments[1] + c22 * moments[2]) / determinant
    return jnp.stack([first, second, third])


def reference(residual, components, chan_weight, tile_pos, facet_psf, psf_spectra):
    channel = jnp.arange(CHAN, dtype=jnp.int32).astype(jnp.float32)
    freqs = (2.0 * channel - (CHAN - 1)) / CHAN
    comp_full = components.astype(jnp.float32)
    powers = [chan_weight, chan_weight * freqs, chan_weight * freqs * freqs]
    moments = jnp.stack([jnp.einsum('c,tcrs->trs', power, comp_full, precision=lax.Precision.HIGHEST) for power in powers])
    gram_terms = jnp.stack([jnp.sum(powers[0]), jnp.sum(powers[1]), jnp.sum(powers[2]),
                            jnp.sum(powers[2] * freqs), jnp.sum(powers[2] * freqs * freqs)])
    coefficients = solve_fit(moments, gram_terms).astype(jnp.bfloat16).astype(jnp.float32)
    model = (coefficients[0][:, None] + coefficients[1][:, None] * freqs[None, :, None, None]
             + coefficients[2][:, None] * (freqs * freqs)[None, :, None, None]).astype(jnp.bfloat16).astype(jnp.float32)
    inv_cos, inv_sin = phase_table(PAD + jnp.arange(FS, dtype=jnp.int32))
    inv_re = inv_cos.astype(jnp.bfloat16).astype(jnp.float32)
    inv_im = inv_sin.astype(jnp.bfloat16).astype(jnp.float32)
    local_pixels = jnp.arange(TS, dtype=jnp.int32)
    high = lax.Precision.HIGHEST

    def one_facet(facet):
        offset_rows = tile_pos[:, 0] - (facet // FCOLS) * FS + PAD
        offset_cols = tile_pos[:, 1] - (facet % FCOLS) * FS + PAD
        inside = ((offset_rows >= 0) & (offset_rows <= FRAME - TS) & (offset_cols >= 0)
                  & (offset_cols <= FRAME - TS)).astype(jnp.float32)[:, None, None]
        col_cos, col_sin = phase_table(offset_cols[:, None] + local_pixels[None, :])
        col_re = col_cos.astype(jnp.bfloat16).astype(jnp.float32)
        col_im = (-col_sin).astype(jnp.bfloat16).astype(jnp.float32)
        row_cos, row_sin = phase_table(offset_rows[:, None] + local_pixels[None, :])
        row_re = (row_cos * inside).astype(jnp.bfloat16).astype(jnp.float32)
        row_im = (-row_sin * inside).astype(jnp.bfloat16).astype(jnp.float32)
        u_re = jnp.einsum('tcrs,tsl->tcrl', model, col_re, precision=high).astype(jnp.bfloat16).astype(jnp.float32)
        u_im = jnp.einsum('tcrs,tsl->tcrl', model, col_im, precision=high).astype(jnp.bfloat16).astype(jnp.float32)
        spec_re = (jnp.einsum('trk,tcrl->ckl', row_re, u_re, precision=high)
                   - jnp.einsum('trk,tcrl->ckl', row_im, u_im, precision=high))
        spec_im = (jnp.einsum('trk,tcrl->ckl', row_re, u_im, precision=high)
                   + jnp.einsum('trk,tcrl->ckl', row_im, u_re, precision=high))
        chosen = psf_spectra[facet_psf[facet]].astype(jnp.float32)
        prod_re = (spec_re * chosen[:, 0] - spec_im * chosen[:, 1]).astype(jnp.bfloat16).astype(jnp.float32)
        prod_im = (spec_re * chosen[:, 1] + spec_im * chosen[:, 0]).astype(jnp.bfloat16).astype(jnp.float32)
        v_re = (jnp.einsum('yk,ckl->cyl', inv_re, prod_re, precision=high)
                - jnp.einsum('yk,ckl->cyl', inv_im, prod_im, precision=high)).astype(jnp.bfloat16).astype(jnp.float32)
        v_im = (jnp.einsum('yk,ckl->cyl', inv_re, prod_im, precision=high)
                + jnp.einsum('yk,ckl->cyl', inv_im, prod_re, precision=high)).astype(jnp.bfloat16).astype(jnp.float32)
        convolved = (jnp.einsum('cyl,xl->cyx', v_re, inv_re, precision=high)
                     - jnp.einsum('cyl,xl->cyx', v_im, inv_im, precision=high)) / (FRAME * FRAME)
        return residual[:, facet] - convolved

    result = lax.map(one_facet, jnp.arange(FACETS, dtype=jnp.int32))
    return jnp.transpose(result, (1, 0, 2, 3))
```

```python
import functools
import math

import jax
import jax.numpy as jnp
from jax import lax
from jax.experimental import pallas as pl
from jax.experimental.pallas import tpu as pltpu
from jax.sharding import PartitionSpec as P

FCOLS = 4


def frequency(chan, total):
    return (2.0 * chan.astype(jnp.float32) - (total - 1)) * (1.0 / total)


def moments_kernel(total, weight_ref, comp_ref, out_ref):
    ntile, nch = comp_ref.shape[:2]
    first = lax.axis_index("freq") * nch
    power = [[], [], []]
    gram = [jnp.float32(0.0)] * 5
    for c in range(nch):
        x = frequency(first + c, total)
        w = weight_ref[c]
        terms = (w, w * x, w * x * x)
        for j in range(3):
            power[j].append(terms[j])
            gram[j] = gram[j] + terms[j]
        gram[3] = gram[3] + terms[2] * x
        gram[4] = gram[4] + terms[2] * x * x
    for t in range(ntile):
        acc = [None] * 3
        for c in range(nch):
            comp = comp_ref[t, c].astype(jnp.float32)
            for j in range(3):
                term = power[j][c] * comp
                acc[j] = term if c == 0 else acc[j] + term
        for j in range(3):
            out_ref[j * ntile + t] = acc[j]
    for j in range(5):
        out_ref[3 * ntile, j : j + 1] = jnp.full((1, out_ref.shape[2]), gram[j], jnp.float32)
    rest = out_ref.shape[1] - 5
    out_ref[3 * ntile, 5:] = jnp.zeros((rest, out_ref.shape[2]), jnp.float32)


def solve_kernel(one_ref, two_ref, out_ref):
    ntile = out_ref.shape[1]
    gram = one_ref[3 * ntile] + two_ref[3 * ntile]
    g0, g1, g2, g3, g4 = (gram[j : j + 1] for j in range(5))
    c00 = g2 * g4 - g3 * g3
    c01 = g2 * g3 - g1 * g4
    c02 = g1 * g3 - g2 * g2
    c11 = g0 * g4 - g2 * g2
    c12 = g1 * g2 - g0 * g3
    c22 = g0 * g2 - g1 * g1
    det = g0 * c00 + g1 * c01 + g2 * c02
    for t in range(ntile):
        m0, m1, m2 = (one_ref[j * ntile + t] + two_ref[j * ntile + t] for j in range(3))
        out_ref[0, t] = ((c00 * m0 + c01 * m1 + c02 * m2) / det).astype(jnp.bfloat16)
        out_ref[1, t] = ((c01 * m0 + c11 * m1 + c12 * m2) / det).astype(jnp.bfloat16)
        out_ref[2, t] = ((c02 * m0 + c12 * m1 + c22 * m2) / det).astype(jnp.bfloat16)


def rows_kernel(total, nch, chan0, psf_of_ref, coef_ref, row_ref, col_ref, inv_ref, psf_ref, *rest):
    out_refs, (lhs_ref, q_ref) = rest[:-2], rest[-2:]
    ntile, ts = coef_ref.shape[1], coef_ref.shape[3]
    na = row_ref.shape[0]
    kb = psf_ref.shape[3]
    frame = psf_ref.shape[4]
    width = ntile * ts
    step = pl.program_id(1)

    @pl.when(step == 0)
    def _():
        x = frequency(lax.axis_index("freq") * nch + chan0 + pl.program_id(0), total)
        for t in range(ntile):
            a0, a1, a2 = (coef_ref[j, t].astype(jnp.float32) for j in range(3))
            model = (a0 + a1 * x + a2 * (x * x)).astype(jnp.bfloat16)
            cols = slice(t * ts, (t + 1) * ts)
            turn = slice(width + t * ts, width + (t + 1) * ts)
            for a in range(na):
                y = jnp.dot(row_ref[a, t], model, preferred_element_type=jnp.float32)
                re, im = y[:kb].astype(jnp.bfloat16), y[kb:].astype(jnp.bfloat16)
                top = slice(a * 2 * kb, a * 2 * kb + kb)
                low = slice(a * 2 * kb + kb, (a + 1) * 2 * kb)
                lhs_ref[top, cols] = re
                lhs_ref[top, turn] = -im
                lhs_ref[low, cols] = im
                lhs_ref[low, turn] = re

    spectrum = jnp.dot(lhs_ref[...], col_ref[0], preferred_element_type=jnp.float32)
    me = lax.axis_index("facet")
    for a in range(na):
        psf = psf_of_ref[jnp.bitwise_xor(me, a * FCOLS + step)]
        p_re = psf_ref[psf, 0, 0].astype(jnp.float32)
        p_im = psf_ref[psf, 0, 1].astype(jnp.float32)
        top = slice(a * 2 * kb, a * 2 * kb + kb)
        low = slice(a * 2 * kb + kb, (a + 1) * 2 * kb)
        s_re, s_im = spectrum[top], spectrum[low]
        q_re = (s_re * p_re - s_im * p_im).astype(jnp.bfloat16)
        q_im = (s_re * p_im + s_im * p_re).astype(jnp.bfloat16)
        q_ref[top, :frame] = q_re
        q_ref[top, frame:] = -q_im
        q_ref[low, :frame] = q_im
        q_ref[low, frame:] = q_re
    w = jnp.dot(q_ref[...], inv_ref[...], preferred_element_type=jnp.float32).astype(jnp.bfloat16)
    for b in range(FCOLS):

        @pl.when(step == b)
        def _():
            for a in range(na):
                for p in range(2):
                    start = (2 * a + p) * kb
                    out_refs[a * FCOLS + b][0, p] = w[start : start + kb]


def pixels_kernel(nf, scale, *refs):
    blocks, table_ref, residual_ref, out_ref = refs[:nf], refs[nf], refs[nf + 1], refs[-1]
    w = jnp.concatenate([blocks[j][0, p] for p in range(2) for j in range(nf)], axis=0)
    conv = jnp.dot(table_ref[...], w, preferred_element_type=jnp.float32)
    out_ref[0, 0] = residual_ref[0, 0] - conv * scale


def turns(index, frame):
    theta = (index % frame).astype(jnp.float32) * (2.0 * math.pi / frame)
    return jnp.cos(theta), jnp.sin(theta)


def chunks_of(nch):
    sizes = [1, 1] if nch >= 2 else []
    left = nch - sum(sizes)
    while left > 0:
        sizes.append(min(1, left))
        left -= sizes[-1]
    starts, at = [], 0
    for s in sizes:
        starts.append((at, s))
        at += s
    return starts


VMEM_LIMIT = 40 * 1024 * 1024


def shards(nf, nz, residual, components, chan_weight, tile_pos, facet_psf, psf_spectra):
    ntile, nch, rows, ts = components.shape
    npsf, _, _, kb, frame = psf_spectra.shape
    fs = residual.shape[2]
    pad = (frame - fs) // 2
    total = nch * nz
    na = nf // FCOLS
    quarter = frame // 4
    bf16, f32, i32 = jnp.bfloat16, jnp.float32, jnp.int32
    me = lax.axis_index("facet")

    psf_of = lax.all_gather(facet_psf, "facet", axis=0, tiled=True)
    sums = pl.pallas_call(
        functools.partial(moments_kernel, total),
        out_shape=jax.ShapeDtypeStruct((3 * ntile + 1, rows, ts), f32),
        in_specs=[pl.BlockSpec(memory_space=pltpu.SMEM), pl.BlockSpec(memory_space=pltpu.VMEM)],
        out_specs=pl.BlockSpec(memory_space=pltpu.VMEM),
        name="moments",
    )(chan_weight, components)
    hops = [1 << i for i in range(nz.bit_length() - 1)]
    other = jnp.zeros_like(sums)
    for i, hop in enumerate(hops):
        if i:
            sums = sums + other
        other = lax.ppermute(sums, "freq", [(s, s ^ hop) for s in range(nz)])
    coefficients = pl.pallas_call(
        solve_kernel,
        out_shape=jax.ShapeDtypeStruct((3, ntile, rows, ts), bf16),
        in_specs=[pl.BlockSpec(memory_space=pltpu.VMEM)] * 2,
        out_specs=pl.BlockSpec(memory_space=pltpu.VMEM),
        name="solve",
    )(sums, other)
    coefficients = lax.all_gather(coefficients, "facet", axis=2, tiled=True)

    a_of = (me // FCOLS) ^ jnp.arange(na, dtype=i32)
    b_of = (me % FCOLS) ^ jnp.arange(FCOLS, dtype=i32)
    oy = tile_pos[None, :, 0] - a_of[:, None] * fs + pad
    ox = tile_pos[None, :, 1] - b_of[:, None] * fs + pad
    row_ok = ((oy >= 0) & (oy <= frame - ts)).astype(f32)
    col_ok = ((ox >= 0) & (ox <= frame - ts)).astype(f32)
    parts = jnp.arange(2, dtype=i32)
    pixel = jnp.arange(ts, dtype=i32)
    freq = jnp.arange(frame, dtype=i32)
    own = me * kb + jnp.arange(kb, dtype=i32)
    index = (oy[:, :, None, None, None] + pixel) * own[:, None] + quarter * parts[:, None, None]
    row_table = (turns(index, frame)[0] * row_ok[:, :, None, None, None]).astype(bf16)
    row_table = row_table.reshape(na, ntile, 2 * kb, ts)
    ca, sa = turns(ox[:, None, :, None] * freq + quarter * parts[:, None, None], frame)
    cb, sb = turns(pixel[:, None] * freq, frame)
    ca = (ca * col_ok[:, None, :, None])[:, :, :, None, :]
    sa = (sa * col_ok[:, None, :, None])[:, :, :, None, :]
    col_table = (ca * cb - sa * sb).astype(bf16).reshape(FCOLS, 2 * ntile * ts, frame)
    place = pad + jnp.arange(fs, dtype=i32)
    fine = 32
    ce, se = turns(fine * jnp.arange(frame // fine, dtype=i32)[:, None] * place - quarter * parts[:, None, None], frame)
    cf, sf = turns(jnp.arange(fine, dtype=i32)[:, None] * place, frame)
    inv_table = (ce[:, :, None, :] * cf - se[:, :, None, :] * sf).astype(bf16).reshape(2 * frame, fs)
    blocks = me ^ jnp.arange(nf, dtype=i32)
    cg, sg = turns(kb * blocks[:, None] * place + quarter * parts[:, None, None], frame)
    ch, sh = turns(jnp.arange(kb, dtype=i32)[:, None] * place, frame)
    pix_table = (cg[:, :, None, :] * ch - sg[:, :, None, :] * sh).astype(bf16).reshape(2 * frame, fs).T

    result = None
    order = sorted(range(1, nf), key=lambda j: -j)
    pieces = []
    for chan0, count in chunks_of(nch):
        w = pl.pallas_call(
            functools.partial(rows_kernel, total, nch, chan0),
            grid_spec=pltpu.PrefetchScalarGridSpec(
                num_scalar_prefetch=1,
                grid=(count, FCOLS),
                in_specs=[
                    pl.BlockSpec((3, ntile, ts, ts), lambda c, b, s: (0, 0, 0, 0)),
                    pl.BlockSpec((na, ntile, 2 * kb, ts), lambda c, b, s: (0, 0, 0, 0)),
                    pl.BlockSpec((1, 2 * ntile * ts, frame), lambda c, b, s: (b, 0, 0)),
                    pl.BlockSpec((2 * frame, fs), lambda c, b, s: (0, 0)),
                    pl.BlockSpec((npsf, 1, 2, kb, frame), lambda c, b, s, c0=chan0: (0, c0 + c, 0, 0, 0)),
                ],
                out_specs=[pl.BlockSpec((1, 2, kb, fs), lambda c, b, s: (c, 0, 0, 0))] * nf,
                scratch_shapes=[
                    pltpu.VMEM((na * 2 * kb, 2 * ntile * ts), bf16),
                    pltpu.VMEM((na * 2 * kb, 2 * frame), bf16),
                ],
            ),
            out_shape=[jax.ShapeDtypeStruct((count, 2, kb, fs), bf16)] * nf,
            cost_estimate=pl.CostEstimate(
                flops=count * nf * 2 * kb * 2 * frame * (2 * ntile * ts + 2 * fs),
                bytes_accessed=count * (npsf * 4 * kb * frame + nf * 4 * kb * fs) + 8 * 2 * ntile * ts * frame,
                transcendentals=0,
            ),
            compiler_params=pltpu.CompilerParams(vmem_limit_bytes=VMEM_LIMIT),
            name="rows",
        )(psf_of, coefficients, row_table, col_table, inv_table, psf_spectra)
        got = [w[0]] + [None] * (nf - 1)
        for j in order:
            got[j] = lax.ppermute(w[j], "facet", [(s, s ^ j) for s in range(nf)])
        pieces.append((chan0, count, got))
    for chan0, count, got in pieces:
        image = pl.BlockSpec((1, 1, fs, fs), lambda c, c0=chan0: (c0 + c, 0, 0, 0))
        before = [] if result is None else [result]
        result = pl.pallas_call(
            functools.partial(pixels_kernel, nf, 1.0 / (frame * frame)),
            grid=(count,),
            in_specs=[pl.BlockSpec((1, 2, kb, fs), lambda c: (c, 0, 0, 0))] * nf
            + [pl.BlockSpec((fs, 2 * frame), lambda c: (0, 0)), image]
            + [pl.BlockSpec(memory_space=pl.ANY)] * len(before),
            out_specs=image,
            out_shape=jax.ShapeDtypeStruct(residual.shape, f32),
            input_output_aliases={nf + 2: 0} if before else {},
            cost_estimate=pl.CostEstimate(
                flops=count * 2 * fs * 2 * frame * fs,
                bytes_accessed=count * (nf * 4 * kb * fs + 8 * fs * fs),
                transcendentals=0,
            ),
            compiler_params=pltpu.CompilerParams(vmem_limit_bytes=VMEM_LIMIT),
            name="pixels",
        )(*got, pix_table, residual, *before)
    return result


def solution(mesh):
    placed = (
        P("freq", "facet", None, None),
        P(None, "freq", "facet", None),
        P("freq"),
        P(),
        P("facet"),
        P(None, "freq", None, "facet", None),
    )
    return jax.shard_map(
        functools.partial(shards, mesh.shape["facet"], mesh.shape["freq"]),
        mesh=mesh,
        in_specs=placed,
        out_specs=P("freq", "facet", None, None),
        check_vma=False,
    )
```

```python
import functools
import math

import jax
import jax.numpy as jnp
from jax import lax
from jax.experimental import pallas as pl
from jax.experimental.pallas import tpu as pltpu
from jax.sharding import PartitionSpec as P

FCOLS = 4
VMEM_LIMIT = 40 * 1024 * 1024

bf16, f32, i32 = jnp.bfloat16, jnp.float32, jnp.int32


def frequency(chan, total):
    return (2.0 * chan.astype(f32) - (total - 1)) * (1.0 / total)


def moments_kernel(total, weight_ref, comp_ref, out_ref):
    ntile, nch = comp_ref.shape[:2]
    first = lax.axis_index("freq") * nch
    power = [[], [], []]
    gram = [jnp.float32(0.0)] * 5
    for c in range(nch):
        x = frequency(first + c, total)
        w = weight_ref[c]
        terms = (w, w * x, w * x * x)
        for j in range(3):
            power[j].append(terms[j])
            gram[j] = gram[j] + terms[j]
        gram[3] = gram[3] + terms[2] * x
        gram[4] = gram[4] + terms[2] * x * x
    for t in range(ntile):
        acc = [None] * 3
        for c in range(nch):
            comp = comp_ref[t, c].astype(f32)
            for j in range(3):
                term = power[j][c] * comp
                acc[j] = term if c == 0 else acc[j] + term
        for j in range(3):
            out_ref[j * ntile + t] = acc[j]
    for j in range(5):
        out_ref[3 * ntile, j : j + 1] = jnp.full((1, out_ref.shape[2]), gram[j], f32)
    rest = out_ref.shape[1] - 5
    out_ref[3 * ntile, 5:] = jnp.zeros((rest, out_ref.shape[2]), f32)


def solve_kernel(psf_ref, one_ref, two_ref, out_ref):
    ntile = (out_ref.shape[0] - 1) // 3
    gram = one_ref[3 * ntile] + two_ref[3 * ntile]
    g0, g1, g2, g3, g4 = (gram[j : j + 1] for j in range(5))
    c00 = g2 * g4 - g3 * g3
    c01 = g2 * g3 - g1 * g4
    c02 = g1 * g3 - g2 * g2
    c11 = g0 * g4 - g2 * g2
    c12 = g1 * g2 - g0 * g3
    c22 = g0 * g2 - g1 * g1
    det = g0 * c00 + g1 * c01 + g2 * c02
    for t in range(ntile):
        m0, m1, m2 = (one_ref[j * ntile + t] + two_ref[j * ntile + t] for j in range(3))
        out_ref[t] = ((c00 * m0 + c01 * m1 + c02 * m2) / det).astype(bf16)
        out_ref[ntile + t] = ((c01 * m0 + c11 * m1 + c12 * m2) / det).astype(bf16)
        out_ref[2 * ntile + t] = ((c02 * m0 + c12 * m1 + c22 * m2) / det).astype(bf16)
    out_ref[3 * ntile] = jnp.full(out_ref.shape[1:], psf_ref[0].astype(f32), f32).astype(bf16)


def cos_turn(index, frame):
    rest = jnp.abs(index - frame * jnp.floor(index * (1.0 / frame) + 0.5))
    x = (frame // 4 - rest) * (2.0 * math.pi / frame)
    square = x * x
    poly = jnp.full_like(square, 1.0 / math.factorial(13))
    for n in (11, 9, 7, 5, 3, 1):
        poly = poly * square + (-1.0) ** ((n - 1) // 2) / math.factorial(n)
    return poly * x


def lane(shape, axis):
    return lax.broadcasted_iota(i32, shape, axis)


def phases_kernel(frame, fs, pos_ref, row_ref, col_ref, inv_ref, flip_ref):
    na, ntile, two_kb, ts = row_ref.shape
    kb = two_kb // 2
    half, quarter, pad = frame // 2, frame // 4, (frame - fs) // 2
    me = lax.axis_index("facet")
    a_me, b_me = lax.div(me, FCOLS), lax.rem(me, FCOLS)
    pixel = lane((1, ts), 1)
    own = (me * kb + lane((kb, 1), 0)).astype(f32)
    for a in range(na):
        for t in range(ntile):
            oy = pos_ref[t, 0] - jnp.bitwise_xor(a_me, a) * fs + pad
            ok = jnp.where((oy >= 0) & (oy <= frame - ts), 1.0, 0.0).astype(f32)
            index = own * (oy + pixel).astype(f32)
            row_ref[a, t, :kb] = (cos_turn(index, frame) * ok).astype(bf16)
            row_ref[a, t, kb:] = (cos_turn(index + quarter, frame) * ok).astype(bf16)
    spot = lane((1, 2 * half), 1)
    freq = jnp.where(spot > half, spot - half, spot).astype(f32)
    shift = jnp.where(spot > half, quarter, 0).astype(f32)
    down = lane((ts, 1), 0)

    def columns(i, carry):
        b, t = lax.div(i, ntile), lax.rem(i, ntile)
        ox = pos_ref[t, 1] - jnp.bitwise_xor(b_me, b) * fs + pad
        ok = jnp.where((ox >= 0) & (ox <= frame - ts), 1.0, 0.0).astype(f32)
        index = (ox + down).astype(f32) * freq + shift
        col_ref[i] = (cos_turn(index, frame) * ok).astype(bf16)
        return carry

    lax.fori_loop(0, FCOLS * ntile, columns, 0)
    place = (pad + lane((1, fs), 1)).astype(f32)
    block = half // 4

    def inverse(i, carry):
        spot = i * block + lane((block, 1), 0)
        freq = jnp.where(spot > half, spot - half, spot).astype(f32)
        shift = jnp.where(spot > half, -quarter, 0).astype(f32)
        inv_ref[pl.ds(i * block, block)] = cos_turn(freq * place + shift, frame).astype(bf16)
        return carry

    lax.fori_loop(0, 8, inverse, 0)
    source = lax.rem(half - lane((1, half), 1), half)
    flip_ref[...] = jnp.where(lane((half, half), 0) == source, 1.0, 0.0).astype(bf16)


def pixel_phases_kernel(frame, pad, nf, out_ref):
    kb = frame // nf
    me = lax.axis_index("facet")
    column = lane((1, 2 * frame), 1)
    k = jnp.zeros((1, 2 * frame), i32)
    for p in range(2):
        for j in range(nf):
            start = p * frame + j * kb
            here = (column >= start) & (column < start + kb)
            k = jnp.where(here, column - start + jnp.bitwise_xor(me, j) * kb, k)
    shift = jnp.where(column >= frame, frame // 4, 0).astype(f32)
    k = k.astype(f32)
    block = 64

    def some(i, carry):
        place = (pad + i * block + lane((block, 1), 0)).astype(f32)
        out_ref[pl.ds(i * block, block)] = cos_turn(place * k + shift, frame).astype(bf16)
        return carry

    lax.fori_loop(0, out_ref.shape[0] // block, some, 0)


def rows_kernel(total, nch, chan0, psf_of_ref, coef_ref, row_ref, col_ref, inv_ref, flip_ref, psf_ref, *rest):
    out_refs, (lhs_ref, rev_ref, q_ref) = rest[:-3], rest[-3:]
    na, ntile, _, ts = row_ref.shape
    nf = coef_ref.shape[0]
    npsf, kb, frame = psf_ref.shape[0], psf_ref.shape[3], psf_ref.shape[4]
    half = frame // 2
    step = pl.program_id(1)

    @pl.when(step == 0)
    def _():
        x = frequency(lax.axis_index("freq") * nch + chan0 + pl.program_id(0), total)
        for t in range(ntile):
            a0, a1, a2 = (
                jnp.concatenate([coef_ref[f, j * ntile + t].astype(f32) for f in range(nf)], axis=0)
                for j in range(3)
            )
            model = (a0 + a1 * x + a2 * (x * x)).astype(bf16)
            for a in range(na):
                y = jnp.dot(row_ref[a, t], model, preferred_element_type=f32)
                lhs_ref[a * 2 * kb : (a + 1) * 2 * kb, t * ts : (t + 1) * ts] = y.astype(bf16)
        for p in range(npsf):
            for part in range(2):
                turned = jnp.dot(psf_ref[p, 0, part, :, half:], flip_ref[...], preferred_element_type=f32)
                rev_ref[p, part] = turned.astype(bf16)

    both = jnp.dot(lhs_ref[...], col_ref[0], preferred_element_type=f32)
    me = lax.axis_index("facet")
    first = lane((1, half), 1) == 0
    zero = jnp.zeros((kb, half), f32)
    for a in range(na):
        psf = psf_of_ref[jnp.bitwise_xor(me, a * FCOLS + step)]
        top = slice(a * 2 * kb, a * 2 * kb + kb)
        low = slice(a * 2 * kb + kb, (a + 1) * 2 * kb)
        rc, rs = both[top, :half], both[top, half:]
        ic, is_ = both[low, :half], both[low, half:]
        rs0, is0 = jnp.where(first, zero, rs), jnp.where(first, zero, is_)
        up_re, up_im = rc - is0, ic + rs0
        dn_re, dn_im = jnp.where(first, rs, rc + is_), jnp.where(first, is_, ic - rs)
        p_re, p_im = psf_ref[psf, 0, 0, :, :half].astype(f32), psf_ref[psf, 0, 1, :, :half].astype(f32)
        n_re, n_im = rev_ref[psf, 0].astype(f32), rev_ref[psf, 1].astype(f32)
        q_re, q_im = up_re * p_re - up_im * p_im, up_re * p_im + up_im * p_re
        z_re, z_im = dn_re * n_re - dn_im * n_im, dn_re * n_im + dn_im * n_re
        q_ref[top, :half] = (q_re + jnp.where(first, zero, z_re)).astype(bf16)
        q_ref[top, half:] = jnp.where(first, z_re, z_im - q_im).astype(bf16)
        q_ref[low, :half] = (q_im + jnp.where(first, zero, z_im)).astype(bf16)
        q_ref[low, half:] = jnp.where(first, z_im, q_re - z_re).astype(bf16)
    w = jnp.dot(q_ref[...], inv_ref[...], preferred_element_type=f32).astype(bf16)
    for b in range(FCOLS):

        @pl.when(step == b)
        def _():
            for a in range(na):
                for p in range(2):
                    start = (2 * a + p) * kb
                    out_refs[a * FCOLS + b][0, p] = w[start : start + kb]


def pixels_kernel(nf, scale, *refs):
    blocks, table_ref, residual_ref, out_ref = refs[:nf], refs[nf], refs[nf + 1], refs[-1]
    w = jnp.concatenate([blocks[j][0, p] for p in range(2) for j in range(nf)], axis=0)
    conv = jnp.dot(table_ref[...], w, preferred_element_type=f32)
    out_ref[0, 0] = residual_ref[0, 0] - conv * scale


def chunks_of(nch):
    return [(c, 1) for c in range(nch)]


def send_order(nf):
    return sorted(range(1, nf), key=lambda j: (-bin(j >> 1).count("1"), j))


VMEM = pl.BlockSpec(memory_space=pltpu.VMEM)
SMEM = pl.BlockSpec(memory_space=pltpu.SMEM)


def shards(nf, nz, residual, components, chan_weight, tile_pos, facet_psf, psf_spectra):
    ntile, nch, rows, ts = components.shape
    npsf, _, _, kb, frame = psf_spectra.shape
    fs = residual.shape[2]
    pad, half = (frame - fs) // 2, frame // 2
    total = nch * nz
    na = nf // FCOLS

    sums = pl.pallas_call(
        functools.partial(moments_kernel, total),
        out_shape=jax.ShapeDtypeStruct((3 * ntile + 1, rows, ts), f32),
        in_specs=[SMEM, VMEM],
        out_specs=VMEM,
        name="moments",
    )(chan_weight, components)
    row_table, col_table, inv_table, flip = pl.pallas_call(
        functools.partial(phases_kernel, frame, fs),
        out_shape=[
            jax.ShapeDtypeStruct((na, ntile, 2 * kb, ts), bf16),
            jax.ShapeDtypeStruct((FCOLS * ntile, ts, frame), bf16),
            jax.ShapeDtypeStruct((frame, fs), bf16),
            jax.ShapeDtypeStruct((half, half), bf16),
        ],
        in_specs=[SMEM],
        out_specs=[VMEM] * 4,
        compiler_params=pltpu.CompilerParams(vmem_limit_bytes=VMEM_LIMIT),
        name="phases",
    )(tile_pos)
    col_table = col_table.reshape(FCOLS, ntile * ts, frame)
    other = jnp.zeros_like(sums)
    for i in range(nz.bit_length() - 1):
        if i:
            sums = sums + other
        other = lax.ppermute(sums, "freq", [(s, s ^ (1 << i)) for s in range(nz)])
    fit = pl.pallas_call(
        solve_kernel,
        out_shape=jax.ShapeDtypeStruct((3 * ntile + 1, rows, ts), bf16),
        in_specs=[SMEM, VMEM, VMEM],
        out_specs=VMEM,
        name="solve",
    )(facet_psf, sums, other)
    fit = lax.all_gather(fit, "facet", axis=0)
    psf_of = fit[:, 3 * ntile, 0, 0].astype(i32)
    pix_table = pl.pallas_call(
        functools.partial(pixel_phases_kernel, frame, pad, nf),
        out_shape=jax.ShapeDtypeStruct((fs, 2 * frame), bf16),
        out_specs=VMEM,
        name="pixphases",
    )()

    pieces = []
    for chan0, count in chunks_of(nch):
        w = pl.pallas_call(
            functools.partial(rows_kernel, total, nch, chan0),
            grid_spec=pltpu.PrefetchScalarGridSpec(
                num_scalar_prefetch=1,
                grid=(count, FCOLS),
                in_specs=[
                    pl.BlockSpec((nf, 3 * ntile + 1, rows, ts), lambda c, b, s: (0, 0, 0, 0)),
                    pl.BlockSpec((na, ntile, 2 * kb, ts), lambda c, b, s: (0, 0, 0, 0)),
                    pl.BlockSpec((1, ntile * ts, frame), lambda c, b, s: (b, 0, 0)),
                    pl.BlockSpec((frame, fs), lambda c, b, s: (0, 0)),
                    pl.BlockSpec((half, half), lambda c, b, s: (0, 0)),
                    pl.BlockSpec((npsf, 1, 2, kb, frame), lambda c, b, s, c0=chan0: (0, c0 + c, 0, 0, 0)),
                ],
                out_specs=[pl.BlockSpec((1, 2, kb, fs), lambda c, b, s: (c, 0, 0, 0))] * nf,
                scratch_shapes=[
                    pltpu.VMEM((na * 2 * kb, ntile * ts), bf16),
                    pltpu.VMEM((npsf, 2, kb, half), bf16),
                    pltpu.VMEM((na * 2 * kb, frame), bf16),
                ],
            ),
            out_shape=[jax.ShapeDtypeStruct((count, 2, kb, fs), bf16)] * nf,
            cost_estimate=pl.CostEstimate(
                flops=count * nf * 4 * kb * frame * (ntile * ts + fs),
                bytes_accessed=count * (npsf * 4 * kb * frame + nf * 4 * kb * fs) + 8 * ntile * ts * frame,
                transcendentals=0,
            ),
            compiler_params=pltpu.CompilerParams(vmem_limit_bytes=VMEM_LIMIT),
            name="rows",
        )(psf_of, fit, row_table, col_table, inv_table, flip, psf_spectra)
        got = [w[0]] + [None] * (nf - 1)
        for j in send_order(nf):
            got[j] = lax.ppermute(w[j], "facet", [(s, s ^ j) for s in range(nf)])
        pieces.append((chan0, count, got))
    result = None
    for chan0, count, got in pieces:
        image = pl.BlockSpec((1, 1, fs, fs), lambda c, c0=chan0: (c0 + c, 0, 0, 0))
        before = [] if result is None else [result]
        result = pl.pallas_call(
            functools.partial(pixels_kernel, nf, 1.0 / (frame * frame)),
            grid=(count,),
            in_specs=[pl.BlockSpec((1, 2, kb, fs), lambda c: (c, 0, 0, 0))] * nf
            + [pl.BlockSpec((fs, 2 * frame), lambda c: (0, 0)), image]
            + [pl.BlockSpec(memory_space=pl.ANY)] * len(before),
            out_specs=image,
            out_shape=jax.ShapeDtypeStruct(residual.shape, f32),
            input_output_aliases={nf + 2: 0} if before else {},
            cost_estimate=pl.CostEstimate(
                flops=count * 4 * fs * frame * fs,
                bytes_accessed=count * (nf * 4 * kb * fs + 8 * fs * fs),
                transcendentals=0,
            ),
            compiler_params=pltpu.CompilerParams(vmem_limit_bytes=VMEM_LIMIT),
            name="pixels",
        )(*got, pix_table, residual, *before)
    return result


def solution(mesh):
    placed = (
        P("freq", "facet", None, None),
        P(None, "freq", "facet", None),
        P("freq"),
        P(),
        P("facet"),
        P(None, "freq", None, "facet", None),
    )
    nf, nz = mesh.shape["facet"], mesh.shape["freq"]

    def step(*args):
        return shards(nf, nz, *args)

    return jax.shard_map(
        step,
        mesh=mesh,
        in_specs=placed,
        out_specs=P("freq", "facet", None, None),
        check_vma=False,
    )
```

```python
import functools
import math

import jax
import jax.numpy as jnp
from jax import lax
from jax.experimental import pallas as pl
from jax.experimental.pallas import tpu as pltpu
from jax.sharding import PartitionSpec as P

FCOLS = 4
VMEM_LIMIT = 20 * 1024 * 1024
SMALL_LIMIT = 12 * 1024 * 1024

bf16, f32, i32 = jnp.bfloat16, jnp.float32, jnp.int32


def frequency(chan, total):
    return (2.0 * chan.astype(f32) - (total - 1)) * (1.0 / total)


def moments_kernel(total, weight_ref, comp_ref, out_ref):
    ntile, nch = comp_ref.shape[:2]
    first = lax.axis_index("freq") * nch
    power = [[], [], []]
    gram = [jnp.float32(0.0)] * 5
    for c in range(nch):
        x = frequency(first + c, total)
        w = weight_ref[c]
        terms = (w, w * x, w * x * x)
        for j in range(3):
            power[j].append(terms[j])
            gram[j] = gram[j] + terms[j]
        gram[3] = gram[3] + terms[2] * x
        gram[4] = gram[4] + terms[2] * x * x
    for t in range(ntile):
        acc = [None] * 3
        for c in range(nch):
            comp = comp_ref[t, c].astype(f32)
            for j in range(3):
                term = power[j][c] * comp
                acc[j] = term if c == 0 else acc[j] + term
        for j in range(3):
            out_ref[j * ntile + t] = acc[j]
    for j in range(5):
        out_ref[3 * ntile, j : j + 1] = jnp.full((1, out_ref.shape[2]), gram[j], f32)
    rest = out_ref.shape[1] - 5
    out_ref[3 * ntile, 5:] = jnp.zeros((rest, out_ref.shape[2]), f32)


def solve_kernel(psf_ref, one_ref, two_ref, out_ref):
    ntile = (out_ref.shape[0] - 1) // 3
    gram = one_ref[3 * ntile] + two_ref[3 * ntile]
    g0, g1, g2, g3, g4 = (gram[j : j + 1] for j in range(5))
    c00 = g2 * g4 - g3 * g3
    c01 = g2 * g3 - g1 * g4
    c02 = g1 * g3 - g2 * g2
    c11 = g0 * g4 - g2 * g2
    c12 = g1 * g2 - g0 * g3
    c22 = g0 * g2 - g1 * g1
    det = g0 * c00 + g1 * c01 + g2 * c02
    for t in range(ntile):
        m0, m1, m2 = (one_ref[j * ntile + t] + two_ref[j * ntile + t] for j in range(3))
        out_ref[t] = ((c00 * m0 + c01 * m1 + c02 * m2) / det).astype(bf16)
        out_ref[ntile + t] = ((c01 * m0 + c11 * m1 + c12 * m2) / det).astype(bf16)
        out_ref[2 * ntile + t] = ((c02 * m0 + c12 * m1 + c22 * m2) / det).astype(bf16)
    out_ref[3 * ntile] = jnp.full(out_ref.shape[1:], psf_ref[0].astype(f32), f32).astype(bf16)


def cos_turn(index, frame):
    rest = jnp.abs(index - frame * jnp.floor(index * (1.0 / frame) + 0.5))
    x = (frame // 4 - rest) * (2.0 * math.pi / frame)
    square = x * x
    poly = jnp.full_like(square, 1.0 / math.factorial(13))
    for n in (11, 9, 7, 5, 3, 1):
        poly = poly * square + (-1.0) ** ((n - 1) // 2) / math.factorial(n)
    return poly * x


def lane(shape, axis):
    return lax.broadcasted_iota(i32, shape, axis)


def row_phases_kernel(frame, fs, pos_ref, row_ref, inv_ref, flip_ref):
    na, ntile, two_kb, ts = row_ref.shape
    kb = two_kb // 2
    half, quarter, pad = frame // 2, frame // 4, (frame - fs) // 2
    me = lax.axis_index("facet")
    a_me = lax.div(me, FCOLS)
    pixel = lane((1, ts), 1)
    own = (me * kb + lane((kb, 1), 0)).astype(f32)
    for a in range(na):
        for t in range(ntile):
            oy = pos_ref[t, 0] - jnp.bitwise_xor(a_me, a) * fs + pad
            ok = jnp.where((oy >= 0) & (oy <= frame - ts), 1.0, 0.0).astype(f32)
            index = own * (oy + pixel).astype(f32)
            row_ref[a, t, :kb] = (cos_turn(index, frame) * ok).astype(bf16)
            row_ref[a, t, kb:] = (cos_turn(index + quarter, frame) * ok).astype(bf16)
    place = (pad + lane((1, fs), 1)).astype(f32)
    block = half // 4

    def inverse(i, carry):
        spot = i * block + lane((block, 1), 0)
        freq = jnp.where(spot > half, spot - half, spot).astype(f32)
        shift = jnp.where(spot > half, -quarter, 0).astype(f32)
        inv_ref[pl.ds(i * block, block)] = cos_turn(freq * place + shift, frame).astype(bf16)
        return carry

    lax.fori_loop(0, 8, inverse, 0)
    source = lax.rem(half - lane((1, half), 1), half)
    flip_ref[...] = jnp.where(lane((half, half), 0) == source, 1.0, 0.0).astype(bf16)


def column_phases_kernel(frame, fs, pos_ref, col_ref, cos_ref, sin_ref):
    ntile, ts = pos_ref.shape[0], col_ref.shape[1]
    half, quarter, pad = frame // 2, frame // 4, (frame - fs) // 2
    b_me = lax.rem(lax.axis_index("facet"), FCOLS)
    spot = lane((1, 2 * half), 1)
    freq = jnp.where(spot > half, spot - half, spot).astype(f32)
    shift = jnp.where(spot > half, quarter, 0).astype(f32)
    grain = lane((ts, 1), 0).astype(f32) * freq
    cos_ref[...] = cos_turn(grain, frame)
    sin_ref[...] = cos_turn(grain - quarter, frame)

    def columns(i, carry):
        b, t = lax.div(i, ntile), lax.rem(i, ntile)
        ox = pos_ref[t, 1] - jnp.bitwise_xor(b_me, b) * fs + pad
        ok = jnp.where((ox >= 0) & (ox <= frame - ts), 1.0, 0.0).astype(f32)
        index = ox.astype(f32) * freq + shift
        cos_ox, sin_ox = cos_turn(index, frame) * ok, cos_turn(index - quarter, frame) * ok
        col_ref[i] = (cos_ox * cos_ref[...] - sin_ox * sin_ref[...]).astype(bf16)
        return carry

    lax.fori_loop(0, FCOLS * ntile, columns, 0)


def pixel_phases_kernel(frame, pad, nf, out_ref):
    kb = frame // nf
    me = lax.axis_index("facet")
    column = lane((1, 2 * frame), 1)
    k = jnp.zeros((1, 2 * frame), i32)
    for p in range(2):
        for j in range(nf):
            start = p * frame + j * kb
            here = (column >= start) & (column < start + kb)
            k = jnp.where(here, column - start + jnp.bitwise_xor(me, j) * kb, k)
    shift = jnp.where(column >= frame, frame // 4, 0).astype(f32)
    k = k.astype(f32)
    block = 64

    def some(i, carry):
        place = (pad + i * block + lane((block, 1), 0)).astype(f32)
        out_ref[pl.ds(i * block, block)] = cos_turn(place * k + shift, frame).astype(bf16)
        return carry

    lax.fori_loop(0, out_ref.shape[0] // block, some, 0)


def rows_kernel(total, nch, chan0, b0, psf_of_ref, coef_ref, row_ref, col_ref, inv_ref, flip_ref, psf_ref, *rest):
    out_refs, (lhs_ref, rev_ref, q_ref) = rest[:-3], rest[-3:]
    na, ntile, _, ts = row_ref.shape
    nf = coef_ref.shape[0]
    npsf, kb, frame = psf_ref.shape[0], psf_ref.shape[3], psf_ref.shape[4]
    half = frame // 2
    step = pl.program_id(1)

    @pl.when(step == 0)
    def _():
        x = frequency(lax.axis_index("freq") * nch + chan0 + pl.program_id(0), total)
        for t in range(ntile):
            a0, a1, a2 = (
                jnp.concatenate([coef_ref[f, j * ntile + t].astype(f32) for f in range(nf)], axis=0)
                for j in range(3)
            )
            model = (a0 + a1 * x + a2 * (x * x)).astype(bf16)
            for a in range(na):
                y = jnp.dot(row_ref[a, t], model, preferred_element_type=f32)
                lhs_ref[a * 2 * kb : (a + 1) * 2 * kb, t * ts : (t + 1) * ts] = y.astype(bf16)
        for p in range(npsf):
            for part in range(2):
                turned = jnp.dot(psf_ref[p, 0, part, :, half:], flip_ref[...], preferred_element_type=f32)
                rev_ref[p, part] = turned.astype(bf16)

    both = jnp.dot(lhs_ref[...], col_ref[0], preferred_element_type=f32)
    me = lax.axis_index("facet")
    first = lane((1, half), 1) == 0
    zero = jnp.zeros((kb, half), f32)
    for a in range(na):
        psf = psf_of_ref[jnp.bitwise_xor(me, a * FCOLS + b0 + step)]
        top = slice(a * 2 * kb, a * 2 * kb + kb)
        low = slice(a * 2 * kb + kb, (a + 1) * 2 * kb)
        rc, rs = both[top, :half], both[top, half:]
        ic, is_ = both[low, :half], both[low, half:]
        rs0, is0 = jnp.where(first, zero, rs), jnp.where(first, zero, is_)
        up_re, up_im = rc - is0, ic + rs0
        dn_re, dn_im = jnp.where(first, rs, rc + is_), jnp.where(first, is_, ic - rs)
        p_re, p_im = psf_ref[psf, 0, 0, :, :half].astype(f32), psf_ref[psf, 0, 1, :, :half].astype(f32)
        n_re, n_im = rev_ref[psf, 0].astype(f32), rev_ref[psf, 1].astype(f32)
        q_re, q_im = up_re * p_re - up_im * p_im, up_re * p_im + up_im * p_re
        z_re, z_im = dn_re * n_re - dn_im * n_im, dn_re * n_im + dn_im * n_re
        q_ref[top, :half] = (q_re + jnp.where(first, zero, z_re)).astype(bf16)
        q_ref[top, half:] = jnp.where(first, z_re, z_im - q_im).astype(bf16)
        q_ref[low, :half] = (q_im + jnp.where(first, zero, z_im)).astype(bf16)
        q_ref[low, half:] = jnp.where(first, z_im, q_re - z_re).astype(bf16)
    w = jnp.dot(q_ref[...], inv_ref[...], preferred_element_type=f32).astype(bf16)
    width = len(out_refs) // na
    for b in range(width):

        @pl.when(step == b)
        def _():
            for a in range(na):
                for p in range(2):
                    start = (2 * a + p) * kb
                    out_refs[a * width + b][0, p] = w[start : start + kb]


def pixels_kernel(nf, scale, *refs):
    blocks, table_ref, residual_ref, out_ref = refs[:nf], refs[nf], refs[nf + 1], refs[-1]
    w = jnp.concatenate([blocks[j][0, p] for p in range(2) for j in range(nf)], axis=0)
    conv = jnp.dot(table_ref[...], w, preferred_element_type=f32)
    out_ref[0, 0] = residual_ref[0, 0] - conv * scale


def chunks_of(nch):
    sizes, left = [], nch
    while left:
        sizes.append(2 if len(sizes) >= 2 and left > 3 else 1)
        left -= sizes[-1]
    return [(sum(sizes[:i]), n, [(0, FCOLS)]) for i, n in enumerate(sizes)]


def send_order(members):
    return sorted((j for j in members if j), key=lambda j: (-bin(j >> 1).count("1"), j))


VMEM = pl.BlockSpec(memory_space=pltpu.VMEM)
SMEM = pl.BlockSpec(memory_space=pltpu.SMEM)


def in_hbm(x):
    return pltpu.with_memory_space_constraint(x, pltpu.HBM)


def shards(nf, nz, residual, components, chan_weight, tile_pos, facet_psf, psf_spectra):
    residual, psf_spectra = in_hbm(residual), in_hbm(psf_spectra)
    ntile, nch, rows, ts = components.shape
    npsf, _, _, kb, frame = psf_spectra.shape
    fs = residual.shape[2]
    pad, half = (frame - fs) // 2, frame // 2
    total = nch * nz
    na = nf // FCOLS

    sums = pl.pallas_call(
        functools.partial(moments_kernel, total),
        out_shape=jax.ShapeDtypeStruct((3 * ntile + 1, rows, ts), f32),
        in_specs=[SMEM, VMEM],
        out_specs=VMEM,
        name="moments",
    )(chan_weight, components)
    row_table, inv_table, flip = pl.pallas_call(
        functools.partial(row_phases_kernel, frame, fs),
        out_shape=[
            jax.ShapeDtypeStruct((na, ntile, 2 * kb, ts), bf16),
            jax.ShapeDtypeStruct((frame, fs), bf16),
            jax.ShapeDtypeStruct((half, half), bf16),
        ],
        in_specs=[SMEM],
        out_specs=[VMEM] * 3,
        compiler_params=pltpu.CompilerParams(vmem_limit_bytes=SMALL_LIMIT),
        name="rowphases",
    )(tile_pos)
    col_table = pl.pallas_call(
        functools.partial(column_phases_kernel, frame, fs),
        out_shape=jax.ShapeDtypeStruct((FCOLS * ntile, ts, frame), bf16),
        in_specs=[SMEM],
        out_specs=VMEM,
        scratch_shapes=[pltpu.VMEM((ts, frame), f32)] * 2,
        compiler_params=pltpu.CompilerParams(vmem_limit_bytes=SMALL_LIMIT),
        name="colphases",
    )(tile_pos)
    row_table, inv_table, flip = in_hbm(row_table), in_hbm(inv_table), in_hbm(flip)
    col_table = col_table.reshape(FCOLS, ntile * ts, frame)
    other = jnp.zeros_like(sums)
    for i in range(nz.bit_length() - 1):
        if i:
            sums = sums + other
        other = lax.ppermute(sums, "freq", [(s, s ^ (1 << i)) for s in range(nz)])
    fit = pl.pallas_call(
        solve_kernel,
        out_shape=jax.ShapeDtypeStruct((3 * ntile + 1, rows, ts), bf16),
        in_specs=[SMEM, VMEM, VMEM],
        out_specs=VMEM,
        name="solve",
    )(facet_psf, sums, other)
    fit = lax.all_gather(fit, "facet", axis=0)
    psf_of = fit[:, 3 * ntile, 0, 0].astype(i32)
    pix_table = pl.pallas_call(
        functools.partial(pixel_phases_kernel, frame, pad, nf),
        out_shape=jax.ShapeDtypeStruct((fs, 2 * frame), bf16),
        out_specs=VMEM,
        name="pixphases",
    )()

    pieces = []
    for chan0, count, groups in chunks_of(nch):
        got = [None] * nf
        for b0, width in groups:
            members = [a * FCOLS + b0 + b for a in range(na) for b in range(width)]
            w = pl.pallas_call(
                functools.partial(rows_kernel, total, nch, chan0, b0),
                grid_spec=pltpu.PrefetchScalarGridSpec(
                    num_scalar_prefetch=1,
                    grid=(count, width),
                    in_specs=[
                        pl.BlockSpec((nf, 3 * ntile + 1, rows, ts), lambda c, b, s: (0, 0, 0, 0)),
                        pl.BlockSpec((na, ntile, 2 * kb, ts), lambda c, b, s: (0, 0, 0, 0)),
                        pl.BlockSpec((1, ntile * ts, frame), lambda c, b, s, b0=b0: (b0 + b, 0, 0)),
                        pl.BlockSpec((frame, fs), lambda c, b, s: (0, 0)),
                        pl.BlockSpec((half, half), lambda c, b, s: (0, 0)),
                        pl.BlockSpec((npsf, 1, 2, kb, frame), lambda c, b, s, c0=chan0: (0, c0 + c, 0, 0, 0)),
                    ],
                    out_specs=[pl.BlockSpec((1, 2, kb, fs), lambda c, b, s: (c, 0, 0, 0))] * (na * width),
                    scratch_shapes=[
                        pltpu.VMEM((na * 2 * kb, ntile * ts), bf16),
                        pltpu.VMEM((npsf, 2, kb, half), bf16),
                        pltpu.VMEM((na * 2 * kb, frame), bf16),
                    ],
                ),
                out_shape=[jax.ShapeDtypeStruct((count, 2, kb, fs), bf16)] * (na * width),
                cost_estimate=pl.CostEstimate(
                    flops=count * na * width * 4 * kb * frame * (ntile * ts + fs),
                    bytes_accessed=count * (npsf * 4 * kb * frame + na * width * 4 * kb * fs)
                    + 2 * width * ntile * ts * frame,
                    transcendentals=0,
                ),
                compiler_params=pltpu.CompilerParams(vmem_limit_bytes=VMEM_LIMIT),
                name="rows",
            )(psf_of, fit, row_table, col_table, inv_table, flip, psf_spectra)
            for i, j in enumerate(members):
                got[j] = w[i]
            for j in send_order(members):
                got[j] = lax.ppermute(got[j], "facet", [(s, s ^ j) for s in range(nf)])
        pieces.append((chan0, count, got))
    result = None
    for chan0, count, got in pieces:
        image = pl.BlockSpec((1, 1, fs, fs), lambda c, c0=chan0: (c0 + c, 0, 0, 0))
        before = [] if result is None else [result]
        result = pl.pallas_call(
            functools.partial(pixels_kernel, nf, 1.0 / (frame * frame)),
            grid=(count,),
            in_specs=[pl.BlockSpec((1, 2, kb, fs), lambda c: (c, 0, 0, 0))] * nf
            + [pl.BlockSpec((fs, 2 * frame), lambda c: (0, 0)), image]
            + [pl.BlockSpec(memory_space=pl.ANY)] * len(before),
            out_specs=image,
            out_shape=jax.ShapeDtypeStruct(residual.shape, f32),
            input_output_aliases={nf + 2: 0} if before else {},
            cost_estimate=pl.CostEstimate(
                flops=count * 4 * fs * frame * fs,
                bytes_accessed=count * (nf * 4 * kb * fs + 8 * fs * fs),
                transcendentals=0,
            ),
            compiler_params=pltpu.CompilerParams(vmem_limit_bytes=VMEM_LIMIT),
            name="pixels",
        )(*got, pix_table, residual, *before)
    return result


def solution(mesh):
    placed = (
        P("freq", "facet", None, None),
        P(None, "freq", "facet", None),
        P("freq"),
        P(),
        P("facet"),
        P(None, "freq", None, "facet", None),
    )
    nf, nz = mesh.shape["facet"], mesh.shape["freq"]

    def step(*args):
        return shards(nf, nz, *args)

    return jax.shard_map(
        step,
        mesh=mesh,
        in_specs=placed,
        out_specs=P("freq", "facet", None, None),
        check_vma=False,
    )
```

```python
import functools
import math

import jax
import jax.numpy as jnp
from jax import lax
from jax.experimental import pallas as pl
from jax.experimental.pallas import tpu as pltpu
from jax.sharding import PartitionSpec as P

FCOLS = 4
VMEM_LIMIT = 20 * 1024 * 1024
SMALL_LIMIT = 12 * 1024 * 1024

bf16, f32, i32 = jnp.bfloat16, jnp.float32, jnp.int32


def frequency(chan, total):
    return (2.0 * chan.astype(f32) - (total - 1)) * (1.0 / total)


def moments_kernel(total, weight_ref, comp_ref, out_ref):
    ntile, nch = comp_ref.shape[:2]
    first = lax.axis_index("freq") * nch
    power = [[], [], []]
    gram = [jnp.float32(0.0)] * 5
    for c in range(nch):
        x = frequency(first + c, total)
        w = weight_ref[c]
        terms = (w, w * x, w * x * x)
        for j in range(3):
            power[j].append(terms[j])
            gram[j] = gram[j] + terms[j]
        gram[3] = gram[3] + terms[2] * x
        gram[4] = gram[4] + terms[2] * x * x
    for t in range(ntile):
        acc = [None] * 3
        for c in range(nch):
            comp = comp_ref[t, c].astype(f32)
            for j in range(3):
                term = power[j][c] * comp
                acc[j] = term if c == 0 else acc[j] + term
        for j in range(3):
            out_ref[j * ntile + t] = acc[j]
    for j in range(5):
        out_ref[3 * ntile, j : j + 1] = jnp.full((1, out_ref.shape[2]), gram[j], f32)
    rest = out_ref.shape[1] - 5
    out_ref[3 * ntile, 5:] = jnp.zeros((rest, out_ref.shape[2]), f32)


def solve_kernel(psf_ref, one_ref, two_ref, out_ref):
    ntile = (out_ref.shape[0] - 1) // 3
    gram = one_ref[3 * ntile] + two_ref[3 * ntile]
    g0, g1, g2, g3, g4 = (gram[j : j + 1] for j in range(5))
    c00 = g2 * g4 - g3 * g3
    c01 = g2 * g3 - g1 * g4
    c02 = g1 * g3 - g2 * g2
    c11 = g0 * g4 - g2 * g2
    c12 = g1 * g2 - g0 * g3
    c22 = g0 * g2 - g1 * g1
    det = g0 * c00 + g1 * c01 + g2 * c02
    for t in range(ntile):
        m0, m1, m2 = (one_ref[j * ntile + t] + two_ref[j * ntile + t] for j in range(3))
        out_ref[t] = ((c00 * m0 + c01 * m1 + c02 * m2) / det).astype(bf16)
        out_ref[ntile + t] = ((c01 * m0 + c11 * m1 + c12 * m2) / det).astype(bf16)
        out_ref[2 * ntile + t] = ((c02 * m0 + c12 * m1 + c22 * m2) / det).astype(bf16)
    out_ref[3 * ntile] = jnp.full(out_ref.shape[1:], psf_ref[0].astype(f32), f32).astype(bf16)


def cos_turn(index, frame):
    rest = jnp.abs(index - frame * jnp.floor(index * (1.0 / frame) + 0.5))
    x = (frame // 4 - rest) * (2.0 * math.pi / frame)
    square = x * x
    poly = jnp.full_like(square, 1.0 / math.factorial(13))
    for n in (11, 9, 7, 5, 3, 1):
        poly = poly * square + (-1.0) ** ((n - 1) // 2) / math.factorial(n)
    return poly * x


def lane(shape, axis):
    return lax.broadcasted_iota(i32, shape, axis)


def row_phases_kernel(frame, fs, pos_ref, row_ref, inv_ref, flip_ref):
    na, ntile, two_kb, ts = row_ref.shape
    kb = two_kb // 2
    half, quarter, pad = frame // 2, frame // 4, (frame - fs) // 2
    me = lax.axis_index("facet")
    a_me = lax.div(me, FCOLS)
    pixel = lane((1, ts), 1)
    own = (me * kb + lane((kb, 1), 0)).astype(f32)
    for a in range(na):
        for t in range(ntile):
            oy = pos_ref[0, t] - jnp.bitwise_xor(a_me, a) * fs + pad
            ok = jnp.where((oy >= 0) & (oy <= frame - ts), 1.0, 0.0).astype(f32)
            index = own * (oy + pixel).astype(f32)
            row_ref[a, t, :kb] = (cos_turn(index, frame) * ok).astype(bf16)
            row_ref[a, t, kb:] = (cos_turn(index + quarter, frame) * ok).astype(bf16)
    place = (pad + lane((1, fs), 1)).astype(f32)
    block = half // 4

    def inverse(i, carry):
        spot = i * block + lane((block, 1), 0)
        freq = jnp.where(spot > half, spot - half, spot).astype(f32)
        shift = jnp.where(spot > half, -quarter, 0).astype(f32)
        inv_ref[pl.ds(i * block, block)] = cos_turn(freq * place + shift, frame).astype(bf16)
        return carry

    lax.fori_loop(0, 8, inverse, 0)
    source = lax.rem(half - lane((1, half), 1), half)
    flip_ref[...] = jnp.where(lane((half, half), 0) == source, 1.0, 0.0).astype(bf16)


def column_phases_kernel(frame, fs, pos_ref, col_ref, cos_ref, sin_ref):
    ntile, ts = pos_ref.shape[1], col_ref.shape[1]
    half, quarter, pad = frame // 2, frame // 4, (frame - fs) // 2
    b_me = lax.rem(lax.axis_index("facet"), FCOLS)
    spot = lane((1, 2 * half), 1)
    freq = jnp.where(spot > half, spot - half, spot).astype(f32)
    shift = jnp.where(spot > half, quarter, 0).astype(f32)
    grain = lane((ts, 1), 0).astype(f32) * freq
    cos_ref[...] = cos_turn(grain, frame)
    sin_ref[...] = cos_turn(grain - quarter, frame)

    def columns(i, carry):
        b, t = lax.div(i, ntile), lax.rem(i, ntile)
        ox = pos_ref[1, t] - jnp.bitwise_xor(b_me, b) * fs + pad
        ok = jnp.where((ox >= 0) & (ox <= frame - ts), 1.0, 0.0).astype(f32)
        index = ox.astype(f32) * freq + shift
        cos_ox, sin_ox = cos_turn(index, frame) * ok, cos_turn(index - quarter, frame) * ok
        col_ref[i] = (cos_ox * cos_ref[...] - sin_ox * sin_ref[...]).astype(bf16)
        return carry

    lax.fori_loop(0, FCOLS * ntile, columns, 0)


def pixel_phases_kernel(frame, pad, nf, kb, out_ref):
    me = lax.axis_index("facet")
    width = out_ref.shape[1]
    rows = width // nf
    column = lane((1, width), 1)
    inner, base = column, jnp.zeros((1, width), i32)
    for j in range(nf):
        here = (column >= j * rows) & (column < (j + 1) * rows)
        inner = jnp.where(here, column - j * rows, inner)
        base = jnp.where(here, jnp.bitwise_xor(me, j) * kb, base)
    count = kb if rows == 2 * kb else kb // 2
    k = jnp.where(inner < count, inner, inner - count)
    k = jnp.where(inner < 2 * count, k, count)
    minus_sin = ((inner >= count) & (inner < 2 * count)) | (inner == 2 * count + 1)
    shift = jnp.where(minus_sin, frame // 4, 0).astype(f32)
    k = (base + k).astype(f32)
    block = 64

    def some(i, carry):
        place = (pad + i * block + lane((block, 1), 0)).astype(f32)
        out_ref[pl.ds(i * block, block)] = cos_turn(place * k + shift, frame).astype(bf16)
        return carry

    lax.fori_loop(0, out_ref.shape[0] // block, some, 0)


def rows_kernel(total, nch, chan0, paired, psf_of_ref, coef_ref, row_ref, col_ref, inv_ref, flip_ref, psf_ref, *rest):
    far_ref, rest = (rest[0], rest[1:]) if paired else (None, rest)
    out_refs, (lhs_ref, psf_up_ref, psf_dn_ref, q_ref) = rest[:-4], rest[-4:]
    na, ntile, _, ts = row_ref.shape
    nf = coef_ref.shape[0]
    npsf, kb, frame = psf_ref.shape[0], psf_ref.shape[3], psf_ref.shape[4]
    rb = lhs_ref.shape[0] // (2 * na)
    half = frame // 2
    step = pl.program_id(1)
    first = lane((1, half), 1) == 0

    def turned(x):
        return jnp.dot(x[:, half:], flip_ref[...], preferred_element_type=f32)

    @pl.when(step == 0)
    def _():
        x = frequency(lax.axis_index("freq") * nch + chan0 + pl.program_id(0), total)
        for t in range(ntile):
            a0, a1, a2 = (
                jnp.concatenate([coef_ref[f, j * ntile + t].astype(f32) for f in range(nf)], axis=0)
                for j in range(3)
            )
            model = (a0 + a1 * x + a2 * (x * x)).astype(bf16)
            for a in range(na):
                y = jnp.dot(row_ref[a, t], model, preferred_element_type=f32).astype(bf16)
                start, cols = a * 2 * rb, slice(t * ts, (t + 1) * ts)
                lhs_ref[start : start + rb, cols] = y[:rb]
                lhs_ref[start + rb : start + 2 * rb, cols] = y[kb : kb + rb]
        if paired:
            count = kb // 2
            i, m = lane((rb, count), 0), lane((rb, count), 1)
            mirror = jnp.where((i >= 1) & (i < count) & (m == count - i), 1.0, 0.0).astype(bf16)
        for p in range(npsf):
            for part in range(2):
                psf = psf_ref[p, 0, part, :rb]
                up, dn = psf[:, :half], turned(psf)
                if paired:
                    far = jnp.dot(mirror, far_ref[p, 0, part], preferred_element_type=f32).astype(bf16)
                    far_up, far_dn = far[:, :half].astype(f32), turned(far)
                    sign = 1.0 - 2.0 * part
                    up = up.astype(f32) + sign * jnp.where(first, far_up, far_dn)
                    dn = dn + sign * jnp.where(first, far_dn, far_up)
                psf_up_ref[p, part] = up.astype(psf_up_ref.dtype)
                psf_dn_ref[p, part] = dn.astype(psf_dn_ref.dtype)

    both = jnp.dot(lhs_ref[...], col_ref[0], preferred_element_type=f32)
    me = lax.axis_index("facet")
    zero = jnp.zeros((rb, half), f32)
    for a in range(na):
        psf = psf_of_ref[jnp.bitwise_xor(me, a * FCOLS + step)]
        top = slice(a * 2 * rb, a * 2 * rb + rb)
        low = slice(a * 2 * rb + rb, (a + 1) * 2 * rb)
        rc, rs = both[top, :half], both[top, half:]
        ic, is_ = both[low, :half], both[low, half:]
        rs0, is0 = jnp.where(first, zero, rs), jnp.where(first, zero, is_)
        up_re, up_im = rc - is0, ic + rs0
        dn_re, dn_im = jnp.where(first, rs, rc + is_), jnp.where(first, is_, ic - rs)
        p_re, p_im = psf_up_ref[psf, 0].astype(f32), psf_up_ref[psf, 1].astype(f32)
        n_re, n_im = psf_dn_ref[psf, 0].astype(f32), psf_dn_ref[psf, 1].astype(f32)
        q_re, q_im = up_re * p_re - up_im * p_im, up_re * p_im + up_im * p_re
        z_re, z_im = dn_re * n_re - dn_im * n_im, dn_re * n_im + dn_im * n_re
        q_ref[top, :half] = (q_re + jnp.where(first, zero, z_re)).astype(bf16)
        q_ref[top, half:] = jnp.where(first, z_re, z_im - q_im).astype(bf16)
        q_ref[low, :half] = (q_im + jnp.where(first, zero, z_im)).astype(bf16)
        q_ref[low, half:] = jnp.where(first, z_im, q_re - z_re).astype(bf16)
    w = jnp.dot(q_ref[...], inv_ref[...], preferred_element_type=f32)
    for b in range(FCOLS):

        @pl.when(step == b)
        def _():
            for a in range(na):
                out_ref, start = out_refs[a * FCOLS + b], a * 2 * rb
                if paired:
                    count = kb // 2
                    out_ref[0, :count] = w[start : start + count].astype(bf16)
                    out_ref[0, count : 2 * count] = w[start + rb : start + rb + count].astype(bf16)
                    re, im = start + count, start + rb + count
                    tile = (TILE, w.shape[1])
                    spot = lane(tile, 0)
                    extra = jnp.where(spot == 1, jnp.broadcast_to(w[im : im + 1], tile), 0.0)
                    extra = jnp.where(spot == 0, jnp.broadcast_to(w[re : re + 1], tile), extra)
                    out_ref[0, 2 * count :] = extra.astype(bf16)
                else:
                    out_ref[0] = w[start : start + 2 * rb].astype(bf16)


def pixels_kernel(nf, scale, *refs):
    blocks, table_ref, residual_ref, out_ref = refs[:nf], refs[nf], refs[nf + 1], refs[-1]
    w = jnp.concatenate([block[0] for block in blocks], axis=0)
    conv = jnp.dot(table_ref[...], w, preferred_element_type=f32)
    out_ref[0, 0] = residual_ref[0, 0] - conv * scale


def chunks_of(nch, npair):
    sizes, left = [], nch - npair
    while left:
        sizes.append(2 if len(sizes) >= 2 and left >= 2 else 1)
        left -= sizes[-1]
    paired = [False] * len(sizes)
    while npair:
        sizes.append(min(2, npair))
        npair -= sizes[-1]
        paired.append(True)
    return [(sum(sizes[:i]), n, paired[i]) for i, n in enumerate(sizes)]


def pairs_of(nch, nf, kb, frame):
    return NPAIR if nch >= NPAIR + 4 and frame == nf * kb and kb % (2 * TILE) == 0 else 0


def send_order(nf):
    return sorted(range(1, nf), key=lambda j: (-bin(j >> 1).count("1"), j))


NPAIR = 2
TILE = 16


VMEM = pl.BlockSpec(memory_space=pltpu.VMEM)
SMEM = pl.BlockSpec(memory_space=pltpu.SMEM)


def in_hbm(x):
    return pltpu.with_memory_space_constraint(x, pltpu.HBM)


def shards(nf, nz, residual, components, chan_weight, tile_pos, facet_psf, psf_spectra):
    whole_psf = psf_spectra
    residual, psf_spectra = in_hbm(residual), in_hbm(psf_spectra)
    ntile, nch, rows, ts = components.shape
    npsf, _, _, kb, frame = psf_spectra.shape
    fs = residual.shape[2]
    pad, half = (frame - fs) // 2, frame // 2
    total = nch * nz
    na = nf // FCOLS
    npair, far = pairs_of(nch, nf, kb, frame), None

    if npair:
        far = lax.ppermute(
            whole_psf[:, nch - npair :, :, kb // 2 :], "facet", [(s, nf - 1 - s) for s in range(nf)]
        )
    sums = pl.pallas_call(
        functools.partial(moments_kernel, total),
        out_shape=jax.ShapeDtypeStruct((3 * ntile + 1, rows, ts), f32),
        in_specs=[SMEM, VMEM],
        out_specs=VMEM,
        name="moments",
    )(chan_weight, components)
    row_table, inv_table, flip = pl.pallas_call(
        functools.partial(row_phases_kernel, frame, fs),
        out_shape=[
            jax.ShapeDtypeStruct((na, ntile, 2 * kb, ts), bf16),
            jax.ShapeDtypeStruct((frame, fs), bf16),
            jax.ShapeDtypeStruct((half, half), bf16),
        ],
        in_specs=[SMEM],
        out_specs=[VMEM] * 3,
        compiler_params=pltpu.CompilerParams(vmem_limit_bytes=SMALL_LIMIT),
        name="rowphases",
    )(tile_pos.T)
    col_table = pl.pallas_call(
        functools.partial(column_phases_kernel, frame, fs),
        out_shape=jax.ShapeDtypeStruct((FCOLS * ntile, ts, frame), bf16),
        in_specs=[SMEM],
        out_specs=VMEM,
        scratch_shapes=[pltpu.VMEM((ts, frame), f32)] * 2,
        compiler_params=pltpu.CompilerParams(vmem_limit_bytes=SMALL_LIMIT),
        name="colphases",
    )(tile_pos.T)
    row_table, inv_table, flip = in_hbm(row_table), in_hbm(inv_table), in_hbm(flip)
    col_table = col_table.reshape(FCOLS, ntile * ts, frame)
    other = jnp.zeros_like(sums)
    for i in range(nz.bit_length() - 1):
        if i:
            sums = sums + other
        other = lax.ppermute(sums, "freq", [(s, s ^ (1 << i)) for s in range(nz)])
    fit = pl.pallas_call(
        solve_kernel,
        out_shape=jax.ShapeDtypeStruct((3 * ntile + 1, rows, ts), bf16),
        in_specs=[SMEM, VMEM, VMEM],
        out_specs=VMEM,
        name="solve",
    )(facet_psf, sums, other)
    fit = lax.all_gather(fit, "facet", axis=0)
    psf_of = fit[:, 3 * ntile, 0, 0].astype(i32)
    rb_pair, block_pair = kb // 2 + TILE, kb + TILE
    tables = {}
    for paired in (False, True)[: 1 + bool(npair)]:
        tables[paired] = pl.pallas_call(
            functools.partial(pixel_phases_kernel, frame, pad, nf, kb),
            out_shape=jax.ShapeDtypeStruct((fs, nf * (block_pair if paired else 2 * kb)), bf16),
            out_specs=VMEM,
            name="pixphases",
        )()

    pieces = []
    for chan0, count, paired in chunks_of(nch, npair):
        rb, block = (rb_pair, block_pair) if paired else (kb, 2 * kb)
        psf_type = f32 if paired else bf16
        fixed = lambda *shape: pl.BlockSpec(shape, lambda c, b, s: (0,) * len(shape))
        w = pl.pallas_call(
            functools.partial(rows_kernel, total, nch, chan0, paired),
            grid_spec=pltpu.PrefetchScalarGridSpec(
                num_scalar_prefetch=1,
                grid=(count, FCOLS),
                in_specs=[
                    fixed(nf, 3 * ntile + 1, rows, ts),
                    fixed(na, ntile, 2 * kb, ts),
                    pl.BlockSpec((1, ntile * ts, frame), lambda c, b, s: (b, 0, 0)),
                    fixed(frame, fs),
                    fixed(half, half),
                    pl.BlockSpec((npsf, 1, 2, kb, frame), lambda c, b, s, c0=chan0: (0, c0 + c, 0, 0, 0)),
                ]
                + [
                    pl.BlockSpec(
                        (npsf, 1, 2, kb // 2, frame),
                        lambda c, b, s, c0=chan0 - (nch - npair): (0, c0 + c, 0, 0, 0),
                    )
                ]
                * paired,
                out_specs=[pl.BlockSpec((1, block, fs), lambda c, b, s: (c, 0, 0))] * nf,
                scratch_shapes=[
                    pltpu.VMEM((na * 2 * rb, ntile * ts), bf16),
                    pltpu.VMEM((npsf, 2, rb, half), psf_type),
                    pltpu.VMEM((npsf, 2, rb, half), psf_type),
                    pltpu.VMEM((na * 2 * rb, frame), bf16),
                ],
            ),
            out_shape=[jax.ShapeDtypeStruct((count, block, fs), bf16)] * nf,
            cost_estimate=pl.CostEstimate(
                flops=count * nf * 4 * rb * frame * (ntile * ts + fs),
                bytes_accessed=count * (npsf * 4 * kb * frame + nf * 2 * block * fs) + 8 * ntile * ts * frame,
                transcendentals=0,
            ),
            compiler_params=pltpu.CompilerParams(vmem_limit_bytes=VMEM_LIMIT),
            name="rows",
        )(psf_of, fit, row_table, col_table, inv_table, flip, psf_spectra, *([far] * paired))
        got = list(w)
        for j in send_order(nf):
            got[j] = lax.ppermute(w[j], "facet", [(s, s ^ j) for s in range(nf)])
        pieces.append((chan0, count, block, tables[paired], got))
    result = None
    for chan0, count, block, pix_table, got in pieces:
        image = pl.BlockSpec((1, 1, fs, fs), lambda c, c0=chan0: (c0 + c, 0, 0, 0))
        before = [] if result is None else [result]
        result = pl.pallas_call(
            functools.partial(pixels_kernel, nf, 1.0 / (frame * frame)),
            grid=(count,),
            in_specs=[pl.BlockSpec((1, block, fs), lambda c: (c, 0, 0))] * nf
            + [pl.BlockSpec((fs, nf * block), lambda c: (0, 0)), image]
            + [pl.BlockSpec(memory_space=pl.ANY)] * len(before),
            out_specs=image,
            out_shape=jax.ShapeDtypeStruct(residual.shape, f32),
            input_output_aliases={nf + 2: 0} if before else {},
            cost_estimate=pl.CostEstimate(
                flops=count * 2 * fs * nf * block * fs,
                bytes_accessed=count * (nf * 2 * block * fs + 8 * fs * fs),
                transcendentals=0,
            ),
            compiler_params=pltpu.CompilerParams(vmem_limit_bytes=VMEM_LIMIT),
            name="pixels",
        )(*got, pix_table, residual, *before)
    return result


def solution(mesh):
    placed = (
        P("freq", "facet", None, None),
        P(None, "freq", "facet", None),
        P("freq"),
        P(),
        P("facet"),
        P(None, "freq", None, "facet", None),
    )
    nf, nz = mesh.shape["facet"], mesh.shape["freq"]

    def step(*args):
        return shards(nf, nz, *args)

    return jax.shard_map(
        step,
        mesh=mesh,
        in_specs=placed,
        out_specs=P("freq", "facet", None, None),
        check_vma=False,
    )
```

```python
import functools
import math

import jax
import jax.numpy as jnp
from jax import lax
from jax.experimental import pallas as pl
from jax.experimental.pallas import tpu as pltpu
from jax.sharding import PartitionSpec as P

FCOLS = 4
VMEM_LIMIT = 20 * 1024 * 1024
SMALL_LIMIT = 12 * 1024 * 1024

bf16, f32, i32 = jnp.bfloat16, jnp.float32, jnp.int32


def frequency(chan, total):
    return (2.0 * chan.astype(f32) - (total - 1)) * (1.0 / total)


def moments_kernel(total, weight_ref, comp_ref, out_ref):
    ntile, nch = comp_ref.shape[:2]
    first = lax.axis_index("freq") * nch
    power = [[], [], []]
    gram = [jnp.float32(0.0)] * 5
    for c in range(nch):
        x = frequency(first + c, total)
        w = weight_ref[c]
        terms = (w, w * x, w * x * x)
        for j in range(3):
            power[j].append(terms[j])
            gram[j] = gram[j] + terms[j]
        gram[3] = gram[3] + terms[2] * x
        gram[4] = gram[4] + terms[2] * x * x
    for t in range(ntile):
        acc = [None] * 3
        for c in range(nch):
            comp = comp_ref[t, c].astype(f32)
            for j in range(3):
                term = power[j][c] * comp
                acc[j] = term if c == 0 else acc[j] + term
        for j in range(3):
            out_ref[j * ntile + t] = acc[j]
    for j in range(5):
        out_ref[3 * ntile, j : j + 1] = jnp.full((1, out_ref.shape[2]), gram[j], f32)
    rest = out_ref.shape[1] - 5
    out_ref[3 * ntile, 5:] = jnp.zeros((rest, out_ref.shape[2]), f32)


def solve_kernel(psf_ref, one_ref, two_ref, out_ref):
    ntile = (out_ref.shape[0] - 1) // 3
    gram = one_ref[3 * ntile] + two_ref[3 * ntile]
    g0, g1, g2, g3, g4 = (gram[j : j + 1] for j in range(5))
    c00 = g2 * g4 - g3 * g3
    c01 = g2 * g3 - g1 * g4
    c02 = g1 * g3 - g2 * g2
    c11 = g0 * g4 - g2 * g2
    c12 = g1 * g2 - g0 * g3
    c22 = g0 * g2 - g1 * g1
    det = g0 * c00 + g1 * c01 + g2 * c02
    for t in range(ntile):
        m0, m1, m2 = (one_ref[j * ntile + t] + two_ref[j * ntile + t] for j in range(3))
        out_ref[t] = ((c00 * m0 + c01 * m1 + c02 * m2) / det).astype(bf16)
        out_ref[ntile + t] = ((c01 * m0 + c11 * m1 + c12 * m2) / det).astype(bf16)
        out_ref[2 * ntile + t] = ((c02 * m0 + c12 * m1 + c22 * m2) / det).astype(bf16)
    out_ref[3 * ntile] = jnp.full(out_ref.shape[1:], psf_ref[0].astype(f32), f32).astype(bf16)


def cos_turn(index, frame):
    rest = jnp.abs(index - frame * jnp.floor(index * (1.0 / frame) + 0.5))
    x = (frame // 4 - rest) * (2.0 * math.pi / frame)
    square = x * x
    poly = jnp.full_like(square, 1.0 / math.factorial(13))
    for n in (11, 9, 7, 5, 3, 1):
        poly = poly * square + (-1.0) ** ((n - 1) // 2) / math.factorial(n)
    return poly * x


def lane(shape, axis):
    return lax.broadcasted_iota(i32, shape, axis)


def row_phases_kernel(frame, fs, pos_ref, row_ref, inv_ref, flip_ref):
    na, ntile, two_kb, ts = row_ref.shape
    kb = two_kb // 2
    half, quarter, pad = frame // 2, frame // 4, (frame - fs) // 2
    me = lax.axis_index("facet")
    a_me = lax.div(me, FCOLS)
    pixel = lane((1, ts), 1)
    own = (me * kb + lane((kb, 1), 0)).astype(f32)
    for a in range(na):
        for t in range(ntile):
            oy = pos_ref[0, t] - jnp.bitwise_xor(a_me, a) * fs + pad
            ok = jnp.where((oy >= 0) & (oy <= frame - ts), 1.0, 0.0).astype(f32)
            index = own * (oy + pixel).astype(f32)
            row_ref[a, t, :kb] = (cos_turn(index, frame) * ok).astype(bf16)
            row_ref[a, t, kb:] = (cos_turn(index + quarter, frame) * ok).astype(bf16)
    place = (pad + lane((1, fs), 1)).astype(f32)
    block = half // 4

    def inverse(i, carry):
        spot = i * block + lane((block, 1), 0)
        freq = jnp.where(spot > half, spot - half, spot).astype(f32)
        shift = jnp.where(spot > half, -quarter, 0).astype(f32)
        inv_ref[pl.ds(i * block, block)] = cos_turn(freq * place + shift, frame).astype(bf16)
        return carry

    lax.fori_loop(0, 8, inverse, 0)
    source = lax.rem(half - lane((1, half), 1), half)
    flip_ref[...] = jnp.where(lane((half, half), 0) == source, 1.0, 0.0).astype(bf16)


def column_phases_kernel(frame, fs, pos_ref, col_ref, cos_ref, sin_ref):
    ntile, ts = pos_ref.shape[1], col_ref.shape[1]
    half, quarter, pad = frame // 2, frame // 4, (frame - fs) // 2
    b_me = lax.rem(lax.axis_index("facet"), FCOLS)
    spot = lane((1, 2 * half), 1)
    freq = jnp.where(spot > half, spot - half, spot).astype(f32)
    shift = jnp.where(spot > half, quarter, 0).astype(f32)
    grain = lane((ts, 1), 0).astype(f32) * freq
    cos_ref[...] = cos_turn(grain, frame)
    sin_ref[...] = cos_turn(grain - quarter, frame)

    def columns(i, carry):
        b, t = lax.div(i, ntile), lax.rem(i, ntile)
        ox = pos_ref[1, t] - jnp.bitwise_xor(b_me, b) * fs + pad
        ok = jnp.where((ox >= 0) & (ox <= frame - ts), 1.0, 0.0).astype(f32)
        index = ox.astype(f32) * freq + shift
        cos_ox, sin_ox = cos_turn(index, frame) * ok, cos_turn(index - quarter, frame) * ok
        col_ref[i] = (cos_ox * cos_ref[...] - sin_ox * sin_ref[...]).astype(bf16)
        return carry

    lax.fori_loop(0, FCOLS * ntile, columns, 0)


def pixel_phases_kernel(frame, pad, nf, kb, out_ref, cos_ref, sin_ref):
    me = lax.axis_index("facet")
    width = out_ref.shape[1]
    rows = width // nf
    column = lane((1, width), 1)
    inner, base = column, jnp.zeros((1, width), i32)
    for j in range(nf):
        here = (column >= j * rows) & (column < (j + 1) * rows)
        inner = jnp.where(here, column - j * rows, inner)
        base = jnp.where(here, jnp.bitwise_xor(me, j) * kb, base)
    count = kb if rows == 2 * kb else kb // 2
    k = jnp.where(inner < count, inner, inner - count)
    k = jnp.where(inner < 2 * count, k, count)
    minus_sin = ((inner >= count) & (inner < 2 * count)) | (inner == 2 * count + 1)
    shift = jnp.where(minus_sin, frame // 4, 0).astype(f32)
    k = (base + k).astype(f32)
    block = 64
    grain = lane((block, 1), 0).astype(f32) * k
    cos_ref[...] = cos_turn(grain, frame)
    sin_ref[...] = cos_turn(grain - frame // 4, frame)

    def some(i, carry):
        coarse = (pad + i * block).astype(f32) * k + shift
        cos_i, sin_i = cos_turn(coarse, frame), cos_turn(coarse - frame // 4, frame)
        out_ref[pl.ds(i * block, block)] = (cos_i * cos_ref[...] - sin_i * sin_ref[...]).astype(bf16)
        return carry

    lax.fori_loop(0, out_ref.shape[0] // block, some, 0)


def rows_kernel(total, nch, chan0, paired, psf_of_ref, coef_ref, row_ref, col_ref, inv_ref, flip_ref, psf_ref, *rest):
    far_ref, rest = (rest[0], rest[1:]) if paired else (None, rest)
    out_refs, (lhs_ref, psf_up_ref, psf_dn_ref, q_ref) = rest[:-4], rest[-4:]
    na, ntile, _, ts = row_ref.shape
    nf = coef_ref.shape[0]
    npsf, kb, frame = psf_ref.shape[0], psf_ref.shape[3], psf_ref.shape[4]
    rb = lhs_ref.shape[0] // (2 * na)
    half = frame // 2
    step = pl.program_id(1)
    first = lane((1, half), 1) == 0

    def turned(x):
        return jnp.dot(x[:, half:], flip_ref[...], preferred_element_type=f32)

    @pl.when(step == 0)
    def _():
        x = frequency(lax.axis_index("freq") * nch + chan0 + pl.program_id(0), total)
        for t in range(ntile):
            a0, a1, a2 = (
                jnp.concatenate([coef_ref[f, j * ntile + t].astype(f32) for f in range(nf)], axis=0)
                for j in range(3)
            )
            model = (a0 + a1 * x + a2 * (x * x)).astype(bf16)
            table = row_ref[:, t].reshape(na * 2 * kb, ts)
            y = jnp.dot(table, model, preferred_element_type=f32).astype(bf16)
            for part in range(2 * na):
                lhs_ref[part * rb : (part + 1) * rb, t * ts : (t + 1) * ts] = y[part * kb : part * kb + rb]
        if paired:
            count = kb // 2
            i, m = lane((rb, count), 0), lane((rb, count), 1)
            mirror = jnp.where((i >= 1) & (i < count) & (m == count - i), 1.0, 0.0).astype(bf16)
        parts = 2 * npsf
        psf = psf_ref[:, 0, :, :rb].reshape(parts * rb, frame)
        up, dn = psf[:, :half], turned(psf)
        if paired:
            far = [
                jnp.dot(mirror, far_ref[i // 2, 0, i % 2], preferred_element_type=f32).astype(bf16)
                for i in range(parts)
            ]
            far = jnp.concatenate(far, axis=0)
            far_up, far_dn = far[:, :half].astype(f32), turned(far)
            for i in range(parts):
                rows, sign = slice(i * rb, (i + 1) * rb), 1.0 - 2.0 * (i % 2)
                psf_up_ref[i // 2, i % 2] = up[rows].astype(f32) + sign * jnp.where(first, far_up[rows], far_dn[rows])
                psf_dn_ref[i // 2, i % 2] = dn[rows] + sign * jnp.where(first, far_dn[rows], far_up[rows])
        else:
            psf_up_ref[...] = up.reshape(psf_up_ref.shape)
            psf_dn_ref[...] = dn.astype(bf16).reshape(psf_dn_ref.shape)

    both = jnp.dot(lhs_ref[...], col_ref[step], preferred_element_type=f32)
    me = lax.axis_index("facet")
    zero = jnp.zeros((rb, half), f32)
    for a in range(na):
        psf = psf_of_ref[jnp.bitwise_xor(me, a * FCOLS + step)]
        top = slice(a * 2 * rb, a * 2 * rb + rb)
        low = slice(a * 2 * rb + rb, (a + 1) * 2 * rb)
        rc, rs = both[top, :half], both[top, half:]
        ic, is_ = both[low, :half], both[low, half:]
        rs0, is0 = jnp.where(first, zero, rs), jnp.where(first, zero, is_)
        up_re, up_im = rc - is0, ic + rs0
        dn_re, dn_im = jnp.where(first, rs, rc + is_), jnp.where(first, is_, ic - rs)
        p_re, p_im = psf_up_ref[psf, 0].astype(f32), psf_up_ref[psf, 1].astype(f32)
        n_re, n_im = psf_dn_ref[psf, 0].astype(f32), psf_dn_ref[psf, 1].astype(f32)
        q_re, q_im = up_re * p_re - up_im * p_im, up_re * p_im + up_im * p_re
        z_re, z_im = dn_re * n_re - dn_im * n_im, dn_re * n_im + dn_im * n_re
        q_ref[top, :half] = (q_re + jnp.where(first, zero, z_re)).astype(bf16)
        q_ref[top, half:] = jnp.where(first, z_re, z_im - q_im).astype(bf16)
        q_ref[low, :half] = (q_im + jnp.where(first, zero, z_im)).astype(bf16)
        q_ref[low, half:] = jnp.where(first, z_im, q_re - z_re).astype(bf16)
    w = jnp.dot(q_ref[...], inv_ref[...], preferred_element_type=f32)
    for b in range(FCOLS):

        @pl.when(step == b)
        def _():
            for a in range(na):
                out_ref, start = out_refs[a * FCOLS + b], a * 2 * rb
                if paired:
                    count = kb // 2
                    out_ref[0, :count] = w[start : start + count].astype(bf16)
                    out_ref[0, count : 2 * count] = w[start + rb : start + rb + count].astype(bf16)
                    re, im = start + count, start + rb + count
                    tile = (TILE, w.shape[1])
                    spot = lane(tile, 0)
                    extra = jnp.where(spot == 1, jnp.broadcast_to(w[im : im + 1], tile), 0.0)
                    extra = jnp.where(spot == 0, jnp.broadcast_to(w[re : re + 1], tile), extra)
                    out_ref[0, 2 * count :] = extra.astype(bf16)
                else:
                    out_ref[0] = w[start : start + 2 * rb].astype(bf16)


def pixels_kernel(nf, scale, *refs):
    blocks, table_ref, residual_ref, out_ref = refs[:nf], refs[nf], refs[nf + 1], refs[-1]
    w = jnp.concatenate([block[0] for block in blocks], axis=0)
    conv = jnp.dot(table_ref[...], w, preferred_element_type=f32)
    out_ref[0, 0] = residual_ref[0, 0] - conv * scale


def chunks_of(nch, npair):
    sizes, left = [], nch - npair
    while left:
        sizes.append(2 if len(sizes) >= 2 and left >= 2 else 1)
        left -= sizes[-1]
    paired = [False] * len(sizes)
    while npair:
        sizes.append(1)
        npair -= sizes[-1]
        paired.append(True)
    return [(sum(sizes[:i]), n, paired[i]) for i, n in enumerate(sizes)]


def pairs_of(nch, nf, kb, frame):
    return NPAIR if nch >= NPAIR + 4 and frame == nf * kb and kb % (2 * TILE) == 0 else 0


def send_order(nf):
    return sorted(range(1, nf), key=lambda j: (-bin(j >> 1).count("1"), j))


NPAIR = 2
TILE = 16


VMEM = pl.BlockSpec(memory_space=pltpu.VMEM)
SMEM = pl.BlockSpec(memory_space=pltpu.SMEM)


def in_hbm(x):
    return pltpu.with_memory_space_constraint(x, pltpu.HBM)


def shards(nf, nz, residual, components, chan_weight, tile_pos, facet_psf, psf_spectra):
    whole_psf = psf_spectra
    residual, psf_spectra = in_hbm(residual), in_hbm(psf_spectra)
    ntile, nch, rows, ts = components.shape
    npsf, _, _, kb, frame = psf_spectra.shape
    fs = residual.shape[2]
    pad, half = (frame - fs) // 2, frame // 2
    total = nch * nz
    na = nf // FCOLS
    npair = pairs_of(nch, nf, kb, frame)

    far = {}
    for i in range(npair):
        chan = nch - npair + i
        mirror = [(s, nf - 1 - s) for s in range(nf)]
        far[chan] = lax.ppermute(whole_psf[:, chan : chan + 1, :, kb // 2 :], "facet", mirror)
    sums = pl.pallas_call(
        functools.partial(moments_kernel, total),
        out_shape=jax.ShapeDtypeStruct((3 * ntile + 1, rows, ts), f32),
        in_specs=[SMEM, VMEM],
        out_specs=VMEM,
        name="moments",
    )(chan_weight, components)
    row_table, inv_table, flip = pl.pallas_call(
        functools.partial(row_phases_kernel, frame, fs),
        out_shape=[
            jax.ShapeDtypeStruct((na, ntile, 2 * kb, ts), bf16),
            pltpu.HBM((frame, fs), bf16),
            pltpu.HBM((half, half), bf16),
        ],
        grid=(1,),
        in_specs=[SMEM],
        out_specs=[
            VMEM,
            pl.BlockSpec((frame, fs), lambda i: (0, 0)),
            pl.BlockSpec((half, half), lambda i: (0, 0)),
        ],
        compiler_params=pltpu.CompilerParams(vmem_limit_bytes=SMALL_LIMIT),
        name="rowphases",
    )(in_hbm(tile_pos.T))
    col_table = pl.pallas_call(
        functools.partial(column_phases_kernel, frame, fs),
        out_shape=jax.ShapeDtypeStruct((FCOLS * ntile, ts, frame), bf16),
        in_specs=[SMEM],
        out_specs=VMEM,
        scratch_shapes=[pltpu.VMEM((ts, frame), f32)] * 2,
        compiler_params=pltpu.CompilerParams(vmem_limit_bytes=SMALL_LIMIT),
        name="colphases",
    )(in_hbm(tile_pos.T))
    col_table = col_table.reshape(FCOLS, ntile * ts, frame)
    other = jnp.zeros_like(sums)
    for i in range(nz.bit_length() - 1):
        if i:
            sums = sums + other
        other = lax.ppermute(sums, "freq", [(s, s ^ (1 << i)) for s in range(nz)])
    fit = pl.pallas_call(
        solve_kernel,
        out_shape=jax.ShapeDtypeStruct((3 * ntile + 1, rows, ts), bf16),
        in_specs=[SMEM, VMEM, VMEM],
        out_specs=VMEM,
        name="solve",
    )(facet_psf, sums, other)
    fit = lax.all_gather(fit, "facet", axis=0)
    psf_of = fit[:, 3 * ntile, 0, 0].astype(i32)
    rb_pair, block_pair = kb // 2 + TILE, kb + TILE
    tables = {}
    for paired in (False, True)[: 1 + bool(npair)]:
        tables[paired] = pl.pallas_call(
            functools.partial(pixel_phases_kernel, frame, pad, nf, kb),
            out_shape=jax.ShapeDtypeStruct((fs, nf * (block_pair if paired else 2 * kb)), bf16),
            out_specs=VMEM,
            scratch_shapes=[pltpu.VMEM((64, nf * (block_pair if paired else 2 * kb)), f32)] * 2,
            name="pixphases",
        )()

    pieces = []
    for chan0, count, paired in chunks_of(nch, npair):
        rb, block = (rb_pair, block_pair) if paired else (kb, 2 * kb)
        psf_type = f32 if paired else bf16
        w = pl.pallas_call(
            functools.partial(rows_kernel, total, nch, chan0, paired),
            grid_spec=pltpu.PrefetchScalarGridSpec(
                num_scalar_prefetch=1,
                grid=(count, FCOLS),
                in_specs=[
                    VMEM,
                    VMEM,
                    VMEM,
                    pl.BlockSpec((frame, fs), lambda c, b, s: (0, 0)),
                    pl.BlockSpec((half, half), lambda c, b, s: (0, 0)),
                    pl.BlockSpec((npsf, 1, 2, kb, frame), lambda c, b, s, c0=chan0: (0, c0 + c, 0, 0, 0)),
                ]
                + [
                    pl.BlockSpec(
                        (npsf, 1, 2, kb // 2, frame),
                        lambda c, b, s: (0, c, 0, 0, 0),
                    )
                ]
                * paired,
                out_specs=[pl.BlockSpec((1, block, fs), lambda c, b, s: (c, 0, 0))] * nf,
                scratch_shapes=[
                    pltpu.VMEM((na * 2 * rb, ntile * ts), bf16),
                    pltpu.VMEM((npsf, 2, rb, half), psf_type),
                    pltpu.VMEM((npsf, 2, rb, half), psf_type),
                    pltpu.VMEM((na * 2 * rb, frame), bf16),
                ],
            ),
            out_shape=[pltpu.HBM((count, block, fs), bf16)] * nf,
            cost_estimate=pl.CostEstimate(
                flops=count * nf * 4 * rb * frame * (ntile * ts + fs),
                bytes_accessed=count * (npsf * 4 * kb * frame + nf * 2 * block * fs) + 8 * ntile * ts * frame,
                transcendentals=0,
            ),
            compiler_params=pltpu.CompilerParams(vmem_limit_bytes=VMEM_LIMIT),
            name="rows",
        )(psf_of, fit, row_table, col_table, in_hbm(inv_table), in_hbm(flip), psf_spectra, *([in_hbm(far[chan0])] if paired else []))
        got = list(w)
        for j in send_order(nf):
            got[j] = lax.ppermute(w[j], "facet", [(s, s ^ j) for s in range(nf)])
        pieces.append((chan0, count, block, tables[paired], got))
    result = None
    for n, (chan0, count, block, pix_table, got) in enumerate(pieces):
        image = pl.BlockSpec((1, 1, fs, fs), lambda c, c0=chan0: (c0 + c, 0, 0, 0))
        before = [] if result is None else [result]
        result = pl.pallas_call(
            functools.partial(pixels_kernel, nf, 1.0 / (frame * frame)),
            grid=(count,),
            in_specs=[pl.BlockSpec((1, block, fs), lambda c: (c, 0, 0))] * nf
            + [VMEM, image]
            + [pl.BlockSpec(memory_space=pl.ANY)] * len(before),
            out_specs=image,
            out_shape=jax.ShapeDtypeStruct(residual.shape, f32),
            input_output_aliases={nf + 2: 0} if before else {},
            cost_estimate=pl.CostEstimate(
                flops=count * 2 * fs * nf * block * fs,
                bytes_accessed=count * (nf * 2 * block * fs + 8 * fs * fs),
                transcendentals=0,
            ),
            compiler_params=pltpu.CompilerParams(vmem_limit_bytes=VMEM_LIMIT),
            name="pixels",
        )(*(got if n >= len(pieces) - 2 else map(in_hbm, got)), pix_table, residual, *before)
    return result


def solution(mesh):
    placed = (
        P("freq", "facet", None, None),
        P(None, "freq", "facet", None),
        P("freq"),
        P(),
        P("facet"),
        P(None, "freq", None, "facet", None),
    )
    nf, nz = mesh.shape["facet"], mesh.shape["freq"]

    def step(*args):
        return shards(nf, nz, *args)

    return jax.shard_map(
        step,
        mesh=mesh,
        in_specs=placed,
        out_specs=P("freq", "facet", None, None),
        check_vma=False,
    )
```

```python
import functools
import math

import jax
import jax.numpy as jnp
from jax import lax
from jax.experimental import pallas as pl
from jax.experimental.pallas import tpu as pltpu
from jax.sharding import PartitionSpec as P

FCOLS = 4
VMEM_LIMIT = 20 * 1024 * 1024
SMALL_LIMIT = 12 * 1024 * 1024

bf16, f32, i32 = jnp.bfloat16, jnp.float32, jnp.int32


def frequency(chan, total):
    return (2.0 * chan.astype(f32) - (total - 1)) * (1.0 / total)


def moments_kernel(total, weight_ref, comp_ref, out_ref):
    ntile, nch = comp_ref.shape[:2]
    first = lax.axis_index("freq") * nch
    power = [[], [], []]
    gram = [jnp.float32(0.0)] * 5
    for c in range(nch):
        x = frequency(first + c, total)
        w = weight_ref[c]
        terms = (w, w * x, w * x * x)
        for j in range(3):
            power[j].append(terms[j])
            gram[j] = gram[j] + terms[j]
        gram[3] = gram[3] + terms[2] * x
        gram[4] = gram[4] + terms[2] * x * x
    for t in range(ntile):
        acc = [None] * 3
        for c in range(nch):
            comp = comp_ref[t, c].astype(f32)
            for j in range(3):
                term = power[j][c] * comp
                acc[j] = term if c == 0 else acc[j] + term
        for j in range(3):
            out_ref[j * ntile + t] = acc[j]
    for j in range(5):
        out_ref[3 * ntile, j : j + 1] = jnp.full((1, out_ref.shape[2]), gram[j], f32)
    rest = out_ref.shape[1] - 5
    out_ref[3 * ntile, 5:] = jnp.zeros((rest, out_ref.shape[2]), f32)


def solve_kernel(psf_ref, one_ref, two_ref, out_ref):
    ntile = (out_ref.shape[0] - 1) // 3
    gram = one_ref[3 * ntile] + two_ref[3 * ntile]
    g0, g1, g2, g3, g4 = (gram[j : j + 1] for j in range(5))
    c00 = g2 * g4 - g3 * g3
    c01 = g2 * g3 - g1 * g4
    c02 = g1 * g3 - g2 * g2
    c11 = g0 * g4 - g2 * g2
    c12 = g1 * g2 - g0 * g3
    c22 = g0 * g2 - g1 * g1
    det = g0 * c00 + g1 * c01 + g2 * c02
    for t in range(ntile):
        m0, m1, m2 = (one_ref[j * ntile + t] + two_ref[j * ntile + t] for j in range(3))
        out_ref[t] = ((c00 * m0 + c01 * m1 + c02 * m2) / det).astype(bf16)
        out_ref[ntile + t] = ((c01 * m0 + c11 * m1 + c12 * m2) / det).astype(bf16)
        out_ref[2 * ntile + t] = ((c02 * m0 + c12 * m1 + c22 * m2) / det).astype(bf16)
    out_ref[3 * ntile] = jnp.full(out_ref.shape[1:], psf_ref[0].astype(f32), f32).astype(bf16)


def cos_turn(index, frame):
    rest = jnp.abs(index - frame * jnp.floor(index * (1.0 / frame) + 0.5))
    x = (frame // 4 - rest) * (2.0 * math.pi / frame)
    square = x * x
    poly = jnp.full_like(square, 1.0 / math.factorial(13))
    for n in (11, 9, 7, 5, 3, 1):
        poly = poly * square + (-1.0) ** ((n - 1) // 2) / math.factorial(n)
    return poly * x


def lane(shape, axis):
    return lax.broadcasted_iota(i32, shape, axis)


def row_phases_kernel(frame, fs, pos_ref, row_ref, inv_ref, flip_ref):
    na, ntile, two_kb, ts = row_ref.shape
    kb = two_kb // 2
    half, quarter, pad = frame // 2, frame // 4, (frame - fs) // 2
    me = lax.axis_index("facet")
    a_me = lax.div(me, FCOLS)
    pixel = lane((1, ts), 1)
    own = (me * kb + lane((kb, 1), 0)).astype(f32)
    for a in range(na):
        for t in range(ntile):
            oy = pos_ref[0, t] - jnp.bitwise_xor(a_me, a) * fs + pad
            ok = jnp.where((oy >= 0) & (oy <= frame - ts), 1.0, 0.0).astype(f32)
            index = own * (oy + pixel).astype(f32)
            row_ref[a, t, :kb] = (cos_turn(index, frame) * ok).astype(bf16)
            row_ref[a, t, kb:] = (cos_turn(index + quarter, frame) * ok).astype(bf16)
    place = (pad + lane((1, fs), 1)).astype(f32)
    block = half // 4

    def inverse(i, carry):
        spot = i * block + lane((block, 1), 0)
        freq = jnp.where(spot > half, spot - half, spot).astype(f32)
        shift = jnp.where(spot > half, -quarter, 0).astype(f32)
        inv_ref[pl.ds(i * block, block)] = cos_turn(freq * place + shift, frame).astype(bf16)
        return carry

    lax.fori_loop(0, 8, inverse, 0)
    source = lax.rem(half - lane((1, half), 1), half)
    flip_ref[...] = jnp.where(lane((half, half), 0) == source, 1.0, 0.0).astype(bf16)


def column_phases_kernel(frame, fs, pos_ref, col_ref, cos_ref, sin_ref):
    ntile, ts = pos_ref.shape[1], col_ref.shape[1]
    half, quarter, pad = frame // 2, frame // 4, (frame - fs) // 2
    b_me = lax.rem(lax.axis_index("facet"), FCOLS)
    spot = lane((1, 2 * half), 1)
    freq = jnp.where(spot > half, spot - half, spot).astype(f32)
    shift = jnp.where(spot > half, quarter, 0).astype(f32)
    grain = lane((ts, 1), 0).astype(f32) * freq
    cos_ref[...] = cos_turn(grain, frame)
    sin_ref[...] = cos_turn(grain - quarter, frame)

    def columns(i, carry):
        b, t = lax.div(i, ntile), lax.rem(i, ntile)
        ox = pos_ref[1, t] - jnp.bitwise_xor(b_me, b) * fs + pad
        ok = jnp.where((ox >= 0) & (ox <= frame - ts), 1.0, 0.0).astype(f32)
        index = ox.astype(f32) * freq + shift
        cos_ox, sin_ox = cos_turn(index, frame) * ok, cos_turn(index - quarter, frame) * ok
        col_ref[i] = (cos_ox * cos_ref[...] - sin_ox * sin_ref[...]).astype(bf16)
        return carry

    lax.fori_loop(0, FCOLS * ntile, columns, 0)


def pixel_phases_kernel(frame, pad, nf, kb, count, extra, out_ref, cos_ref, sin_ref):
    me = lax.axis_index("facet")
    width = out_ref.shape[1]
    column = lane((1, width), 1)
    inner, base = column, jnp.zeros((1, width), i32)
    for j in range(nf):
        for start, rows, skip in ((j * 2 * count, 2 * count, 0), (nf * 2 * count + j * extra, extra, 2 * count)):
            here = (column >= start) & (column < start + rows)
            inner = jnp.where(here, column - start + skip, inner)
            base = jnp.where(here, jnp.bitwise_xor(me, j) * kb, base)
    k = jnp.where(inner < count, inner, inner - count)
    k = jnp.where(inner < 2 * count, k, count)
    minus_sin = ((inner >= count) & (inner < 2 * count)) | (inner == 2 * count + 1)
    shift = jnp.where(minus_sin, frame // 4, 0).astype(f32)
    k = (base + k).astype(f32)
    block = 64
    grain = lane((block, 1), 0).astype(f32) * k
    cos_ref[...] = cos_turn(grain, frame)
    sin_ref[...] = cos_turn(grain - frame // 4, frame)

    def some(i, carry):
        coarse = (pad + i * block).astype(f32) * k + shift
        cos_i, sin_i = cos_turn(coarse, frame), cos_turn(coarse - frame // 4, frame)
        out_ref[pl.ds(i * block, block)] = (cos_i * cos_ref[...] - sin_i * sin_ref[...]).astype(bf16)
        return carry

    lax.fori_loop(0, out_ref.shape[0] // block, some, 0)


def rows_kernel(total, nch, chan0, paired, psf_of_ref, coef_ref, row_ref, col_ref, inv_ref, flip_ref, psf_ref, *rest):
    far_ref, rest = (rest[0], rest[1:]) if paired else (None, rest)
    out_refs, (lhs_ref, psf_up_ref, psf_dn_ref, q_ref) = rest[:-4], rest[-4:]
    na, ntile, _, ts = row_ref.shape
    nf = coef_ref.shape[0]
    npsf, kb, frame = psf_ref.shape[0], psf_ref.shape[3], psf_ref.shape[4]
    rb = lhs_ref.shape[0] // (2 * na)
    half = frame // 2
    step = pl.program_id(1)
    first = lane((1, half), 1) == 0

    def turned(x):
        return jnp.dot(x[:, half:], flip_ref[...], preferred_element_type=f32)

    @pl.when(step == 0)
    def _():
        x = frequency(lax.axis_index("freq") * nch + chan0 + pl.program_id(0), total)
        for t in range(ntile):
            a0, a1, a2 = (
                jnp.concatenate([coef_ref[f, j * ntile + t].astype(f32) for f in range(nf)], axis=0)
                for j in range(3)
            )
            model = (a0 + a1 * x + a2 * (x * x)).astype(bf16)
            table = row_ref[:, t].reshape(na * 2 * kb, ts)
            y = jnp.dot(table, model, preferred_element_type=f32).astype(bf16)
            for part in range(2 * na):
                lhs_ref[part * rb : (part + 1) * rb, t * ts : (t + 1) * ts] = y[part * kb : part * kb + rb]
        if paired:
            count = kb // 2
            i, m = lane((rb, count), 0), lane((rb, count), 1)
            mirror = jnp.where((i >= 1) & (i < count) & (m == count - i), 1.0, 0.0).astype(bf16)
        parts = 2 * npsf
        psf = psf_ref[:, 0, :, :rb].reshape(parts * rb, frame)
        up, dn = psf[:, :half], turned(psf)
        if paired:
            far = [
                jnp.dot(mirror, far_ref[i // 2, 0, i % 2], preferred_element_type=f32).astype(bf16)
                for i in range(parts)
            ]
            far = jnp.concatenate(far, axis=0)
            far_up, far_dn = far[:, :half].astype(f32), turned(far)
            for i in range(parts):
                rows, sign = slice(i * rb, (i + 1) * rb), 1.0 - 2.0 * (i % 2)
                psf_up_ref[i // 2, i % 2] = up[rows].astype(f32) + sign * jnp.where(first, far_up[rows], far_dn[rows])
                psf_dn_ref[i // 2, i % 2] = dn[rows] + sign * jnp.where(first, far_dn[rows], far_up[rows])
        else:
            psf_up_ref[...] = up.reshape(psf_up_ref.shape)
            psf_dn_ref[...] = dn.astype(bf16).reshape(psf_dn_ref.shape)

    both = jnp.dot(lhs_ref[...], col_ref[step], preferred_element_type=f32)
    me = lax.axis_index("facet")
    zero = jnp.zeros((rb, half), f32)
    for a in range(na):
        psf = psf_of_ref[jnp.bitwise_xor(me, a * FCOLS + step)]
        top = slice(a * 2 * rb, a * 2 * rb + rb)
        low = slice(a * 2 * rb + rb, (a + 1) * 2 * rb)
        rc, rs = both[top, :half], both[top, half:]
        ic, is_ = both[low, :half], both[low, half:]
        rs0, is0 = jnp.where(first, zero, rs), jnp.where(first, zero, is_)
        up_re, up_im = rc - is0, ic + rs0
        dn_re, dn_im = jnp.where(first, rs, rc + is_), jnp.where(first, is_, ic - rs)
        p_re, p_im = psf_up_ref[psf, 0].astype(f32), psf_up_ref[psf, 1].astype(f32)
        n_re, n_im = psf_dn_ref[psf, 0].astype(f32), psf_dn_ref[psf, 1].astype(f32)
        q_re, q_im = up_re * p_re - up_im * p_im, up_re * p_im + up_im * p_re
        z_re, z_im = dn_re * n_re - dn_im * n_im, dn_re * n_im + dn_im * n_re
        q_ref[top, :half] = (q_re + jnp.where(first, zero, z_re)).astype(bf16)
        q_ref[top, half:] = jnp.where(first, z_re, z_im - q_im).astype(bf16)
        q_ref[low, :half] = (q_im + jnp.where(first, zero, z_im)).astype(bf16)
        q_ref[low, half:] = jnp.where(first, z_im, q_re - z_re).astype(bf16)
    w = jnp.dot(q_ref[...], inv_ref[...], preferred_element_type=f32)
    for b in range(FCOLS):

        @pl.when(step == b)
        def _():
            for a in range(na):
                out_ref, start = out_refs[a * FCOLS + b], a * 2 * rb
                if paired:
                    count = kb // 2
                    out_ref[0, :count] = w[start : start + count].astype(bf16)
                    out_ref[0, count : 2 * count] = w[start + rb : start + rb + count].astype(bf16)
                    re, im = start + count, start + rb + count
                    tile = (EXTRA, w.shape[1])
                    spot = lane(tile, 0)
                    extra = jnp.where(spot == 1, jnp.broadcast_to(w[im : im + 1], tile), 0.0)
                    extra = jnp.where(spot == 0, jnp.broadcast_to(w[re : re + 1], tile), extra)
                    out_ref[0, 2 * count :] = extra.astype(bf16)
                else:
                    out_ref[0] = w[start : start + 2 * rb].astype(bf16)


def pixels_kernel(nf, scale, extra, *refs):
    blocks, table_ref, residual_ref, out_ref = refs[:nf], refs[nf], refs[nf + 1], refs[-1]
    rows = blocks[0].shape[1] - extra
    w = jnp.concatenate([block[0, :rows] for block in blocks], axis=0)
    if extra:
        more = jnp.concatenate([block[0, rows:].astype(f32) for block in blocks], axis=0)
        w = jnp.concatenate([w, more.astype(bf16)], axis=0)
    conv = jnp.dot(table_ref[...], w, preferred_element_type=f32)
    out_ref[0, 0] = residual_ref[0, 0] - conv * scale


def chunks_of(nch, npair):
    sizes, left = [], nch - npair
    while left:
        sizes.append(2 if len(sizes) >= 2 and left >= 2 else 1)
        left -= sizes[-1]
    paired = [False] * len(sizes)
    while npair:
        sizes.append(1)
        npair -= sizes[-1]
        paired.append(True)
    return [(sum(sizes[:i]), n, paired[i]) for i, n in enumerate(sizes)]


def pairs_of(nch, nf, kb, frame):
    return NPAIR if nch >= NPAIR + 4 and frame == nf * kb and kb % (2 * TILE) == 0 else 0


def send_order(nf):
    return sorted(range(1, nf), key=lambda j: (-bin(j >> 1).count("1"), j))


NPAIR = 2
TILE = 16
EXTRA = 8


VMEM = pl.BlockSpec(memory_space=pltpu.VMEM)
SMEM = pl.BlockSpec(memory_space=pltpu.SMEM)


def in_hbm(x):
    return pltpu.with_memory_space_constraint(x, pltpu.HBM)


def shards(nf, nz, residual, components, chan_weight, tile_pos, facet_psf, psf_spectra):
    whole_psf = psf_spectra
    residual, psf_spectra = in_hbm(residual), in_hbm(psf_spectra)
    ntile, nch, rows, ts = components.shape
    npsf, _, _, kb, frame = psf_spectra.shape
    fs = residual.shape[2]
    pad, half = (frame - fs) // 2, frame // 2
    total = nch * nz
    na = nf // FCOLS
    npair = pairs_of(nch, nf, kb, frame)

    far = {}
    for i in range(npair):
        chan = nch - npair + i
        mirror = [(s, nf - 1 - s) for s in range(nf)]
        far[chan] = lax.ppermute(whole_psf[:, chan : chan + 1, :, kb // 2 :], "facet", mirror)
    sums = pl.pallas_call(
        functools.partial(moments_kernel, total),
        out_shape=jax.ShapeDtypeStruct((3 * ntile + 1, rows, ts), f32),
        in_specs=[SMEM, VMEM],
        out_specs=VMEM,
        name="moments",
    )(chan_weight, components)
    row_table, inv_table, flip = pl.pallas_call(
        functools.partial(row_phases_kernel, frame, fs),
        out_shape=[
            jax.ShapeDtypeStruct((na, ntile, 2 * kb, ts), bf16),
            pltpu.HBM((frame, fs), bf16),
            pltpu.HBM((half, half), bf16),
        ],
        grid=(1,),
        in_specs=[SMEM],
        out_specs=[
            VMEM,
            pl.BlockSpec((frame, fs), lambda i: (0, 0)),
            pl.BlockSpec((half, half), lambda i: (0, 0)),
        ],
        compiler_params=pltpu.CompilerParams(vmem_limit_bytes=SMALL_LIMIT),
        name="rowphases",
    )(in_hbm(tile_pos.T))
    col_table = pl.pallas_call(
        functools.partial(column_phases_kernel, frame, fs),
        out_shape=jax.ShapeDtypeStruct((FCOLS * ntile, ts, frame), bf16),
        in_specs=[SMEM],
        out_specs=VMEM,
        scratch_shapes=[pltpu.VMEM((ts, frame), f32)] * 2,
        compiler_params=pltpu.CompilerParams(vmem_limit_bytes=SMALL_LIMIT),
        name="colphases",
    )(in_hbm(tile_pos.T))
    col_table = col_table.reshape(FCOLS, ntile * ts, frame)
    other = jnp.zeros_like(sums)
    for i in range(nz.bit_length() - 1):
        if i:
            sums = sums + other
        other = lax.ppermute(sums, "freq", [(s, s ^ (1 << i)) for s in range(nz)])
    fit = pl.pallas_call(
        solve_kernel,
        out_shape=jax.ShapeDtypeStruct((3 * ntile + 1, rows, ts), bf16),
        in_specs=[SMEM, VMEM, VMEM],
        out_specs=VMEM,
        name="solve",
    )(facet_psf, sums, other)
    fit = lax.all_gather(fit, "facet", axis=0)
    psf_of = fit[:, 3 * ntile, 0, 0].astype(i32)
    rb_pair, block_pair = kb // 2 + TILE, kb + EXTRA
    tables = {}
    for paired in (False, True)[: 1 + bool(npair)]:
        tables[paired] = pl.pallas_call(
            functools.partial(
                pixel_phases_kernel, frame, pad, nf, kb, kb // 2 if paired else kb, EXTRA * paired
            ),
            out_shape=jax.ShapeDtypeStruct((fs, nf * (block_pair if paired else 2 * kb)), bf16),
            out_specs=VMEM,
            scratch_shapes=[pltpu.VMEM((64, nf * (block_pair if paired else 2 * kb)), f32)] * 2,
            name="pixphases",
        )()

    pieces = []
    for chan0, count, paired in chunks_of(nch, npair):
        rb, block = (rb_pair, block_pair) if paired else (kb, 2 * kb)
        psf_type = f32 if paired else bf16
        w = pl.pallas_call(
            functools.partial(rows_kernel, total, nch, chan0, paired),
            grid_spec=pltpu.PrefetchScalarGridSpec(
                num_scalar_prefetch=1,
                grid=(count, FCOLS),
                in_specs=[
                    VMEM,
                    VMEM,
                    VMEM,
                    pl.BlockSpec((frame, fs), lambda c, b, s: (0, 0)),
                    pl.BlockSpec((half, half), lambda c, b, s: (0, 0)),
                    pl.BlockSpec((npsf, 1, 2, kb, frame), lambda c, b, s, c0=chan0: (0, c0 + c, 0, 0, 0)),
                ]
                + [
                    pl.BlockSpec(
                        (npsf, 1, 2, kb // 2, frame),
                        lambda c, b, s: (0, c, 0, 0, 0),
                    )
                ]
                * paired,
                out_specs=[pl.BlockSpec((1, block, fs), lambda c, b, s: (c, 0, 0))] * nf,
                scratch_shapes=[
                    pltpu.VMEM((na * 2 * rb, ntile * ts), bf16),
                    pltpu.VMEM((npsf, 2, rb, half), psf_type),
                    pltpu.VMEM((npsf, 2, rb, half), psf_type),
                    pltpu.VMEM((na * 2 * rb, frame), bf16),
                ],
            ),
            out_shape=[pltpu.HBM((count, block, fs), bf16)] * nf,
            cost_estimate=pl.CostEstimate(
                flops=count * nf * 4 * rb * frame * (ntile * ts + fs),
                bytes_accessed=count * (npsf * 4 * kb * frame + nf * 2 * block * fs) + 8 * ntile * ts * frame,
                transcendentals=0,
            ),
            compiler_params=pltpu.CompilerParams(vmem_limit_bytes=VMEM_LIMIT),
            name="rows",
        )(psf_of, fit, row_table, col_table, in_hbm(inv_table), in_hbm(flip), psf_spectra, *([in_hbm(far[chan0])] if paired else []))
        got = list(w)
        for j in send_order(nf):
            got[j] = lax.ppermute(w[j], "facet", [(s, s ^ j) for s in range(nf)])
        pieces.append((chan0, count, block, tables[paired], got))
    result = None
    for n, (chan0, count, block, pix_table, got) in enumerate(pieces):
        image = pl.BlockSpec((1, 1, fs, fs), lambda c, c0=chan0: (c0 + c, 0, 0, 0))
        before = [] if result is None else [result]
        result = pl.pallas_call(
            functools.partial(
                pixels_kernel, nf, 1.0 / (frame * frame), EXTRA if block == block_pair else 0
            ),
            grid=(count,),
            in_specs=[pl.BlockSpec((1, block, fs), lambda c: (c, 0, 0))] * nf
            + [VMEM, image]
            + [pl.BlockSpec(memory_space=pl.ANY)] * len(before),
            out_specs=image,
            out_shape=jax.ShapeDtypeStruct(residual.shape, f32),
            input_output_aliases={nf + 2: 0} if before else {},
            cost_estimate=pl.CostEstimate(
                flops=count * 2 * fs * nf * block * fs,
                bytes_accessed=count * (nf * 2 * block * fs + 8 * fs * fs),
                transcendentals=0,
            ),
            compiler_params=pltpu.CompilerParams(vmem_limit_bytes=VMEM_LIMIT),
            name="pixels",
        )(*(got if n >= len(pieces) - 2 else map(in_hbm, got)), pix_table, residual, *before)
    return result


def solution(mesh):
    placed = (
        P("freq", "facet", None, None),
        P(None, "freq", "facet", None),
        P("freq"),
        P(),
        P("facet"),
        P(None, "freq", None, "facet", None),
    )
    nf, nz = mesh.shape["facet"], mesh.shape["freq"]

    def step(*args):
        return shards(nf, nz, *args)

    return jax.shard_map(
        step,
        mesh=mesh,
        in_specs=placed,
        out_specs=P("freq", "facet", None, None),
        check_vma=False,
    )
```

```python
import functools
import math

import jax
import jax.numpy as jnp
from jax import lax
from jax.experimental import pallas as pl
from jax.experimental.pallas import tpu as pltpu
from jax.sharding import PartitionSpec as P

FCOLS = 4
VMEM_LIMIT = 20 * 1024 * 1024
SMALL_LIMIT = 12 * 1024 * 1024

bf16, f32, i32 = jnp.bfloat16, jnp.float32, jnp.int32


def frequency(chan, total):
    return (2.0 * chan.astype(f32) - (total - 1)) * (1.0 / total)


def moments_kernel(total, weight_ref, comp_ref, out_ref):
    ntile, nch = comp_ref.shape[:2]
    first = lax.axis_index("freq") * nch
    power = [[], [], []]
    gram = [jnp.float32(0.0)] * 5
    for c in range(nch):
        x = frequency(first + c, total)
        w = weight_ref[c]
        terms = (w, w * x, w * x * x)
        for j in range(3):
            power[j].append(terms[j])
            gram[j] = gram[j] + terms[j]
        gram[3] = gram[3] + terms[2] * x
        gram[4] = gram[4] + terms[2] * x * x
    for t in range(ntile):
        acc = [None] * 3
        for c in range(nch):
            comp = comp_ref[t, c].astype(f32)
            for j in range(3):
                term = power[j][c] * comp
                acc[j] = term if c == 0 else acc[j] + term
        for j in range(3):
            out_ref[j * ntile + t] = acc[j]
    for j in range(5):
        out_ref[3 * ntile, j : j + 1] = jnp.full((1, out_ref.shape[2]), gram[j], f32)
    rest = out_ref.shape[1] - 5
    out_ref[3 * ntile, 5:] = jnp.zeros((rest, out_ref.shape[2]), f32)


def total_of(parts):
    while len(parts) > 1:
        parts = [a + b for a, b in zip(parts[::2], parts[1::2])]
    return parts[0]


def solve_kernel(psf_ref, *refs):
    refs, out_ref = refs[:-1], refs[-1]
    ntile = (out_ref.shape[0] - 1) // 3
    gram = total_of([ref[3 * ntile] for ref in refs])
    g0, g1, g2, g3, g4 = (gram[j : j + 1] for j in range(5))
    c00 = g2 * g4 - g3 * g3
    c01 = g2 * g3 - g1 * g4
    c02 = g1 * g3 - g2 * g2
    c11 = g0 * g4 - g2 * g2
    c12 = g1 * g2 - g0 * g3
    c22 = g0 * g2 - g1 * g1
    det = g0 * c00 + g1 * c01 + g2 * c02
    for t in range(ntile):
        m0, m1, m2 = (total_of([ref[j * ntile + t] for ref in refs]) for j in range(3))
        out_ref[t] = ((c00 * m0 + c01 * m1 + c02 * m2) / det).astype(bf16)
        out_ref[ntile + t] = ((c01 * m0 + c11 * m1 + c12 * m2) / det).astype(bf16)
        out_ref[2 * ntile + t] = ((c02 * m0 + c12 * m1 + c22 * m2) / det).astype(bf16)
    out_ref[3 * ntile] = jnp.full(out_ref.shape[1:], psf_ref[0].astype(f32), f32).astype(bf16)


def cos_turn(index, frame):
    rest = jnp.abs(index - frame * jnp.floor(index * (1.0 / frame) + 0.5))
    x = (frame // 4 - rest) * (2.0 * math.pi / frame)
    square = x * x
    poly = jnp.full_like(square, 1.0 / math.factorial(13))
    for n in (11, 9, 7, 5, 3, 1):
        poly = poly * square + (-1.0) ** ((n - 1) // 2) / math.factorial(n)
    return poly * x


def lane(shape, axis):
    return lax.broadcasted_iota(i32, shape, axis)


def row_phases_kernel(frame, fs, pos_ref, row_ref, inv_ref, flip_ref):
    na, ntile, two_kb, ts = row_ref.shape
    kb = two_kb // 2
    half, quarter, pad = frame // 2, frame // 4, (frame - fs) // 2
    me = lax.axis_index("facet")
    a_me = lax.div(me, FCOLS)
    pixel = lane((1, ts), 1)
    own = (me * kb + lane((kb, 1), 0)).astype(f32)
    for a in range(na):
        for t in range(ntile):
            oy = pos_ref[0, t] - jnp.bitwise_xor(a_me, a) * fs + pad
            ok = jnp.where((oy >= 0) & (oy <= frame - ts), 1.0, 0.0).astype(f32)
            index = own * (oy + pixel).astype(f32)
            row_ref[a, t, :kb] = (cos_turn(index, frame) * ok).astype(bf16)
            row_ref[a, t, kb:] = (cos_turn(index + quarter, frame) * ok).astype(bf16)
    place = (pad + lane((1, fs), 1)).astype(f32)
    block = half // 4

    def inverse(i, carry):
        spot = i * block + lane((block, 1), 0)
        freq = jnp.where(spot > half, spot - half, spot).astype(f32)
        shift = jnp.where(spot > half, -quarter, 0).astype(f32)
        inv_ref[pl.ds(i * block, block)] = cos_turn(freq * place + shift, frame).astype(bf16)
        return carry

    lax.fori_loop(0, 8, inverse, 0)
    source = lax.rem(half - lane((1, half), 1), half)
    flip_ref[...] = jnp.where(lane((half, half), 0) == source, 1.0, 0.0).astype(bf16)


def column_phases_kernel(frame, fs, pos_ref, col_ref, cos_ref, sin_ref):
    ntile, ts = pos_ref.shape[1], col_ref.shape[1]
    half, quarter, pad = frame // 2, frame // 4, (frame - fs) // 2
    b_me = lax.rem(lax.axis_index("facet"), FCOLS)
    spot = lane((1, 2 * half), 1)
    freq = jnp.where(spot > half, spot - half, spot).astype(f32)
    shift = jnp.where(spot > half, quarter, 0).astype(f32)
    grain = lane((ts, 1), 0).astype(f32) * freq
    cos_ref[...] = cos_turn(grain, frame)
    sin_ref[...] = cos_turn(grain - quarter, frame)

    def columns(i, carry):
        b, t = lax.div(i, ntile), lax.rem(i, ntile)
        ox = pos_ref[1, t] - jnp.bitwise_xor(b_me, b) * fs + pad
        ok = jnp.where((ox >= 0) & (ox <= frame - ts), 1.0, 0.0).astype(f32)
        index = ox.astype(f32) * freq + shift
        cos_ox, sin_ox = cos_turn(index, frame) * ok, cos_turn(index - quarter, frame) * ok
        col_ref[i] = (cos_ox * cos_ref[...] - sin_ox * sin_ref[...]).astype(bf16)
        return carry

    lax.fori_loop(0, FCOLS * ntile, columns, 0)


def pixel_phases_kernel(frame, pad, nf, kb, count, extra, out_ref, cos_ref, sin_ref):
    me = lax.axis_index("facet")
    width = out_ref.shape[1]
    column = lane((1, width), 1)
    inner, base = column, jnp.zeros((1, width), i32)
    for j in range(nf):
        for start, rows, skip in ((j * 2 * count, 2 * count, 0), (nf * 2 * count + j * extra, extra, 2 * count)):
            here = (column >= start) & (column < start + rows)
            inner = jnp.where(here, column - start + skip, inner)
            base = jnp.where(here, jnp.bitwise_xor(me, j) * kb, base)
    k = jnp.where(inner < count, inner, inner - count)
    k = jnp.where(inner < 2 * count, k, count)
    minus_sin = ((inner >= count) & (inner < 2 * count)) | (inner == 2 * count + 1)
    shift = jnp.where(minus_sin, frame // 4, 0).astype(f32)
    k = (base + k).astype(f32)
    block = 64
    grain = lane((block, 1), 0).astype(f32) * k
    cos_ref[...] = cos_turn(grain, frame)
    sin_ref[...] = cos_turn(grain - frame // 4, frame)

    def some(i, carry):
        coarse = (pad + i * block).astype(f32) * k + shift
        cos_i, sin_i = cos_turn(coarse, frame), cos_turn(coarse - frame // 4, frame)
        out_ref[pl.ds(i * block, block)] = (cos_i * cos_ref[...] - sin_i * sin_ref[...]).astype(bf16)
        return carry

    lax.fori_loop(0, out_ref.shape[0] // block, some, 0)


def rows_kernel(total, nch, chan0, paired, psf_of_ref, coef_ref, row_ref, col_ref, inv_ref, flip_ref, psf_ref, *rest):
    far_ref, rest = (rest[0], rest[1:]) if paired else (None, rest)
    out_refs, (lhs_ref, psf_up_ref, psf_dn_ref, q_ref) = rest[:-4], rest[-4:]
    na, ntile, _, ts = row_ref.shape
    nf = coef_ref.shape[0]
    npsf, kb, frame = psf_ref.shape[0], psf_ref.shape[3], psf_ref.shape[4]
    rb = lhs_ref.shape[0] // (2 * na)
    half = frame // 2
    step = pl.program_id(1)
    first = lane((1, half), 1) == 0

    def turned(x):
        return jnp.dot(x[:, half:], flip_ref[...], preferred_element_type=f32)

    @pl.when(step == 0)
    def _():
        x = frequency(lax.axis_index("freq") * nch + chan0 + pl.program_id(0), total)
        for t in range(ntile):
            a0, a1, a2 = (
                jnp.concatenate([coef_ref[f, j * ntile + t].astype(f32) for f in range(nf)], axis=0)
                for j in range(3)
            )
            model = (a0 + a1 * x + a2 * (x * x)).astype(bf16)
            table = row_ref[:, t].reshape(na * 2 * kb, ts)
            y = jnp.dot(table, model, preferred_element_type=f32).astype(bf16)
            for part in range(2 * na):
                lhs_ref[part * rb : (part + 1) * rb, t * ts : (t + 1) * ts] = y[part * kb : part * kb + rb]
        if paired:
            count = kb // 2
            i, m = lane((rb, count), 0), lane((rb, count), 1)
            mirror = jnp.where((i >= 1) & (i < count) & (m == count - i), 1.0, 0.0).astype(bf16)
        parts = 2 * npsf
        psf = psf_ref[:, 0, :, :rb].reshape(parts * rb, frame)
        up, dn = psf[:, :half], turned(psf)
        if paired:
            far = [
                jnp.dot(mirror, far_ref[i // 2, 0, i % 2], preferred_element_type=f32).astype(bf16)
                for i in range(parts)
            ]
            far = jnp.concatenate(far, axis=0)
            far_up, far_dn = far[:, :half].astype(f32), turned(far)
            for i in range(parts):
                rows, sign = slice(i * rb, (i + 1) * rb), 1.0 - 2.0 * (i % 2)
                psf_up_ref[i // 2, i % 2] = up[rows].astype(f32) + sign * jnp.where(first, far_up[rows], far_dn[rows])
                psf_dn_ref[i // 2, i % 2] = dn[rows] + sign * jnp.where(first, far_dn[rows], far_up[rows])
        else:
            psf_up_ref[...] = up.reshape(psf_up_ref.shape)
            psf_dn_ref[...] = dn.astype(bf16).reshape(psf_dn_ref.shape)

    both = jnp.dot(lhs_ref[...], col_ref[step], preferred_element_type=f32)
    me = lax.axis_index("facet")
    zero = jnp.zeros((rb, half), f32)
    for a in range(na):
        psf = psf_of_ref[jnp.bitwise_xor(me, a * FCOLS + step)]
        top = slice(a * 2 * rb, a * 2 * rb + rb)
        low = slice(a * 2 * rb + rb, (a + 1) * 2 * rb)
        rc, rs = both[top, :half], both[top, half:]
        ic, is_ = both[low, :half], both[low, half:]
        rs0, is0 = jnp.where(first, zero, rs), jnp.where(first, zero, is_)
        up_re, up_im = rc - is0, ic + rs0
        dn_re, dn_im = jnp.where(first, rs, rc + is_), jnp.where(first, is_, ic - rs)
        p_re, p_im = psf_up_ref[psf, 0].astype(f32), psf_up_ref[psf, 1].astype(f32)
        n_re, n_im = psf_dn_ref[psf, 0].astype(f32), psf_dn_ref[psf, 1].astype(f32)
        q_re, q_im = up_re * p_re - up_im * p_im, up_re * p_im + up_im * p_re
        z_re, z_im = dn_re * n_re - dn_im * n_im, dn_re * n_im + dn_im * n_re
        q_ref[top, :half] = (q_re + jnp.where(first, zero, z_re)).astype(bf16)
        q_ref[top, half:] = jnp.where(first, z_re, z_im - q_im).astype(bf16)
        q_ref[low, :half] = (q_im + jnp.where(first, zero, z_im)).astype(bf16)
        q_ref[low, half:] = jnp.where(first, z_im, q_re - z_re).astype(bf16)
    w = jnp.dot(q_ref[...], inv_ref[...], preferred_element_type=f32)
    for b in range(FCOLS):

        @pl.when(step == b)
        def _():
            for a in range(na):
                out_ref, start = out_refs[a * FCOLS + b], a * 2 * rb
                if paired:
                    count = kb // 2
                    out_ref[0, :count] = w[start : start + count].astype(bf16)
                    out_ref[0, count : 2 * count] = w[start + rb : start + rb + count].astype(bf16)
                    re, im = start + count, start + rb + count
                    tile = (EXTRA, w.shape[1])
                    spot = lane(tile, 0)
                    extra = jnp.where(spot == 1, jnp.broadcast_to(w[im : im + 1], tile), 0.0)
                    extra = jnp.where(spot == 0, jnp.broadcast_to(w[re : re + 1], tile), extra)
                    out_ref[0, 2 * count :] = extra.astype(bf16)
                else:
                    out_ref[0] = w[start : start + 2 * rb].astype(bf16)


def pixels_kernel(nf, scale, extra, *refs):
    blocks, table_ref, residual_ref, out_ref = refs[:nf], refs[nf], refs[nf + 1], refs[-1]
    rows = blocks[0].shape[1] - extra
    w = jnp.concatenate([block[0, :rows] for block in blocks], axis=0)
    if extra:
        more = jnp.concatenate([block[0, rows:].astype(f32) for block in blocks], axis=0)
        w = jnp.concatenate([w, more.astype(bf16)], axis=0)
    conv = jnp.dot(table_ref[...], w, preferred_element_type=f32)
    out_ref[0, 0] = residual_ref[0, 0] - conv * scale


def chunks_of(nch, npair):
    sizes, left = [], nch - npair
    while left:
        sizes.append(2 if len(sizes) >= 2 and left >= 2 else 1)
        left -= sizes[-1]
    paired = [False] * len(sizes)
    while npair:
        sizes.append(1)
        npair -= sizes[-1]
        paired.append(True)
    return [(sum(sizes[:i]), n, paired[i]) for i, n in enumerate(sizes)]


def pairs_of(nch, nf, kb, frame):
    return NPAIR if nch >= NPAIR + 4 and frame == nf * kb and kb % (2 * TILE) == 0 else 0


def rounds_of(nz):
    rounds, stride = [], 1
    while stride < nz:
        rounds.append((stride, min(4, nz // stride)))
        stride *= rounds[-1][1]
    return rounds


def send_order(nf):
    return sorted(range(1, nf), key=lambda j: (-bin(j >> 1).count("1"), j))


NPAIR = 2
TILE = 16
EXTRA = 8


VMEM = pl.BlockSpec(memory_space=pltpu.VMEM)
SMEM = pl.BlockSpec(memory_space=pltpu.SMEM)


def in_hbm(x):
    return pltpu.with_memory_space_constraint(x, pltpu.HBM)


def shards(nf, nz, residual, components, chan_weight, tile_pos, facet_psf, psf_spectra):
    whole_psf = psf_spectra
    residual, psf_spectra = in_hbm(residual), in_hbm(psf_spectra)
    ntile, nch, rows, ts = components.shape
    npsf, _, _, kb, frame = psf_spectra.shape
    fs = residual.shape[2]
    pad, half = (frame - fs) // 2, frame // 2
    total = nch * nz
    na = nf // FCOLS
    npair = pairs_of(nch, nf, kb, frame)

    far = {}
    for i in range(npair):
        chan = nch - npair + i
        mirror = [(s, nf - 1 - s) for s in range(nf)]
        far[chan] = lax.ppermute(whole_psf[:, chan : chan + 1, :, kb // 2 :], "facet", mirror)
    sums = pl.pallas_call(
        functools.partial(moments_kernel, total),
        out_shape=jax.ShapeDtypeStruct((3 * ntile + 1, rows, ts), f32),
        in_specs=[SMEM, VMEM],
        out_specs=VMEM,
        name="moments",
    )(chan_weight, components)
    row_table, inv_table, flip = pl.pallas_call(
        functools.partial(row_phases_kernel, frame, fs),
        out_shape=[
            jax.ShapeDtypeStruct((na, ntile, 2 * kb, ts), bf16),
            pltpu.HBM((frame, fs), bf16),
            pltpu.HBM((half, half), bf16),
        ],
        grid=(1,),
        in_specs=[SMEM],
        out_specs=[
            VMEM,
            pl.BlockSpec((frame, fs), lambda i: (0, 0)),
            pl.BlockSpec((half, half), lambda i: (0, 0)),
        ],
        compiler_params=pltpu.CompilerParams(vmem_limit_bytes=SMALL_LIMIT),
        name="rowphases",
    )(in_hbm(tile_pos.T))
    col_table = pl.pallas_call(
        functools.partial(column_phases_kernel, frame, fs),
        out_shape=jax.ShapeDtypeStruct((FCOLS * ntile, ts, frame), bf16),
        in_specs=[SMEM],
        out_specs=VMEM,
        scratch_shapes=[pltpu.VMEM((ts, frame), f32)] * 2,
        compiler_params=pltpu.CompilerParams(vmem_limit_bytes=SMALL_LIMIT),
        name="colphases",
    )(in_hbm(tile_pos.T))
    col_table = col_table.reshape(FCOLS, ntile * ts, frame)
    terms = [sums]
    for stride, size in rounds_of(nz):
        sums = total_of(terms)
        terms = [sums] + [None] * (size - 1)
        for h in range(size - 1, 0, -1):
            terms[h] = lax.ppermute(sums, "freq", [(s, s ^ (stride * h)) for s in range(nz)])
    fit = pl.pallas_call(
        solve_kernel,
        out_shape=jax.ShapeDtypeStruct((3 * ntile + 1, rows, ts), bf16),
        in_specs=[SMEM] + [VMEM] * len(terms),
        out_specs=VMEM,
        name="solve",
    )(facet_psf, *terms)
    fit = lax.all_gather(fit, "facet", axis=0)
    psf_of = fit[:, 3 * ntile, 0, 0].astype(i32)
    rb_pair, block_pair = kb // 2 + TILE, kb + EXTRA
    tables = {}
    for paired in (False, True)[: 1 + bool(npair)]:
        tables[paired] = pl.pallas_call(
            functools.partial(
                pixel_phases_kernel, frame, pad, nf, kb, kb // 2 if paired else kb, EXTRA * paired
            ),
            out_shape=jax.ShapeDtypeStruct((fs, nf * (block_pair if paired else 2 * kb)), bf16),
            out_specs=VMEM,
            scratch_shapes=[pltpu.VMEM((64, nf * (block_pair if paired else 2 * kb)), f32)] * 2,
            name="pixphases",
        )()

    pieces = []
    for chan0, count, paired in chunks_of(nch, npair):
        rb, block = (rb_pair, block_pair) if paired else (kb, 2 * kb)
        psf_type = f32 if paired else bf16
        w = pl.pallas_call(
            functools.partial(rows_kernel, total, nch, chan0, paired),
            grid_spec=pltpu.PrefetchScalarGridSpec(
                num_scalar_prefetch=1,
                grid=(count, FCOLS),
                in_specs=[
                    VMEM,
                    VMEM,
                    VMEM,
                    pl.BlockSpec((frame, fs), lambda c, b, s: (0, 0)),
                    pl.BlockSpec((half, half), lambda c, b, s: (0, 0)),
                    pl.BlockSpec((npsf, 1, 2, kb, frame), lambda c, b, s, c0=chan0: (0, c0 + c, 0, 0, 0)),
                ]
                + [
                    pl.BlockSpec(
                        (npsf, 1, 2, kb // 2, frame),
                        lambda c, b, s: (0, c, 0, 0, 0),
                    )
                ]
                * paired,
                out_specs=[pl.BlockSpec((1, block, fs), lambda c, b, s: (c, 0, 0))] * nf,
                scratch_shapes=[
                    pltpu.VMEM((na * 2 * rb, ntile * ts), bf16),
                    pltpu.VMEM((npsf, 2, rb, half), psf_type),
                    pltpu.VMEM((npsf, 2, rb, half), psf_type),
                    pltpu.VMEM((na * 2 * rb, frame), bf16),
                ],
            ),
            out_shape=[pltpu.HBM((count, block, fs), bf16)] * nf,
            cost_estimate=pl.CostEstimate(
                flops=count * nf * 4 * rb * frame * (ntile * ts + fs),
                bytes_accessed=count * (npsf * 4 * kb * frame + nf * 2 * block * fs) + 8 * ntile * ts * frame,
                transcendentals=0,
            ),
            compiler_params=pltpu.CompilerParams(vmem_limit_bytes=VMEM_LIMIT),
            name="rows",
        )(psf_of, fit, row_table, col_table, in_hbm(inv_table), in_hbm(flip), psf_spectra, *([in_hbm(far[chan0])] if paired else []))
        got = list(w)
        for j in send_order(nf):
            got[j] = lax.ppermute(w[j], "facet", [(s, s ^ j) for s in range(nf)])
        pieces.append((chan0, count, block, tables[paired], got))
    result = None
    for n, (chan0, count, block, pix_table, got) in enumerate(pieces):
        image = pl.BlockSpec((1, 1, fs, fs), lambda c, c0=chan0: (c0 + c, 0, 0, 0))
        before = [] if result is None else [result]
        result = pl.pallas_call(
            functools.partial(
                pixels_kernel, nf, 1.0 / (frame * frame), EXTRA if block == block_pair else 0
            ),
            grid=(count,),
            in_specs=[pl.BlockSpec((1, block, fs), lambda c: (c, 0, 0))] * nf
            + [VMEM, image]
            + [pl.BlockSpec(memory_space=pl.ANY)] * len(before),
            out_specs=image,
            out_shape=jax.ShapeDtypeStruct(residual.shape, f32),
            input_output_aliases={nf + 2: 0} if before else {},
            cost_estimate=pl.CostEstimate(
                flops=count * 2 * fs * nf * block * fs,
                bytes_accessed=count * (nf * 2 * block * fs + 8 * fs * fs),
                transcendentals=0,
            ),
            compiler_params=pltpu.CompilerParams(vmem_limit_bytes=VMEM_LIMIT),
            name="pixels",
        )(*(got if n >= len(pieces) - 2 else map(in_hbm, got)), pix_table, residual, *before)
    return result


def solution(mesh):
    placed = (
        P("freq", "facet", None, None),
        P(None, "freq", "facet", None),
        P("freq"),
        P(),
        P("facet"),
        P(None, "freq", None, "facet", None),
    )
    nf, nz = mesh.shape["facet"], mesh.shape["freq"]

    def step(*args):
        return shards(nf, nz, *args)

    return jax.shard_map(
        step,
        mesh=mesh,
        in_specs=placed,
        out_specs=P("freq", "facet", None, None),
        check_vma=False,
    )
```

```python
import functools
import math

import jax
import jax.numpy as jnp
from jax import lax
from jax.experimental import pallas as pl
from jax.experimental.pallas import tpu as pltpu
from jax.sharding import PartitionSpec as P

FCOLS = 4
VMEM_LIMIT = 20 * 1024 * 1024
SMALL_LIMIT = 10 * 1024 * 1024

bf16, f32, i32 = jnp.bfloat16, jnp.float32, jnp.int32


def frequency(chan, total):
    return (2.0 * chan.astype(f32) - (total - 1)) * (1.0 / total)


def moments_kernel(total, weight_ref, comp_ref, out_ref):
    ntile, nch = comp_ref.shape[:2]
    first = lax.axis_index("freq") * nch
    power = [[], [], []]
    gram = [jnp.float32(0.0)] * 5
    for c in range(nch):
        x = frequency(first + c, total)
        w = weight_ref[c]
        terms = (w, w * x, w * x * x)
        for j in range(3):
            power[j].append(terms[j])
            gram[j] = gram[j] + terms[j]
        gram[3] = gram[3] + terms[2] * x
        gram[4] = gram[4] + terms[2] * x * x
    for t in range(ntile):
        acc = [None] * 3
        for c in range(nch):
            comp = comp_ref[t, c].astype(f32)
            for j in range(3):
                term = power[j][c] * comp
                acc[j] = term if c == 0 else acc[j] + term
        for j in range(3):
            out_ref[j * ntile + t] = acc[j]
    for j in range(5):
        out_ref[3 * ntile, j : j + 1] = jnp.full((1, out_ref.shape[2]), gram[j], f32)
    rest = out_ref.shape[1] - 5
    out_ref[3 * ntile, 5:] = jnp.zeros((rest, out_ref.shape[2]), f32)


def solve_kernel(psf_ref, one_ref, two_ref, out_ref):
    ntile = (out_ref.shape[0] - 1) // 3
    gram = one_ref[3 * ntile] + two_ref[3 * ntile]
    g0, g1, g2, g3, g4 = (gram[j : j + 1] for j in range(5))
    c00 = g2 * g4 - g3 * g3
    c01 = g2 * g3 - g1 * g4
    c02 = g1 * g3 - g2 * g2
    c11 = g0 * g4 - g2 * g2
    c12 = g1 * g2 - g0 * g3
    c22 = g0 * g2 - g1 * g1
    det = g0 * c00 + g1 * c01 + g2 * c02
    for t in range(ntile):
        m0, m1, m2 = (one_ref[j * ntile + t] + two_ref[j * ntile + t] for j in range(3))
        out_ref[t] = ((c00 * m0 + c01 * m1 + c02 * m2) / det).astype(bf16)
        out_ref[ntile + t] = ((c01 * m0 + c11 * m1 + c12 * m2) / det).astype(bf16)
        out_ref[2 * ntile + t] = ((c02 * m0 + c12 * m1 + c22 * m2) / det).astype(bf16)
    out_ref[3 * ntile] = jnp.full(out_ref.shape[1:], psf_ref[0].astype(f32), f32).astype(bf16)


def cos_turn(index, frame):
    rest = jnp.abs(index - frame * jnp.floor(index * (1.0 / frame) + 0.5))
    x = (frame // 4 - rest) * (2.0 * math.pi / frame)
    square = x * x
    poly = jnp.full_like(square, 1.0 / math.factorial(13))
    for n in (11, 9, 7, 5, 3, 1):
        poly = poly * square + (-1.0) ** ((n - 1) // 2) / math.factorial(n)
    return poly * x


def lane(shape, axis):
    return lax.broadcasted_iota(i32, shape, axis)


def row_phases_kernel(frame, fs, pos_ref, row_ref, inv_ref, flip_ref):
    na, ntile, two_kb, ts = row_ref.shape
    kb = two_kb // 2
    half, quarter, pad = frame // 2, frame // 4, (frame - fs) // 2
    me = lax.axis_index("facet")
    a_me = lax.div(me, FCOLS)
    pixel = lane((1, ts), 1)
    own = (me * kb + lane((kb, 1), 0)).astype(f32)
    for a in range(na):
        for t in range(ntile):
            oy = pos_ref[0, t] - jnp.bitwise_xor(a_me, a) * fs + pad
            ok = jnp.where((oy >= 0) & (oy <= frame - ts), 1.0, 0.0).astype(f32)
            index = own * (oy + pixel).astype(f32)
            row_ref[a, t, :kb] = (cos_turn(index, frame) * ok).astype(bf16)
            row_ref[a, t, kb:] = (cos_turn(index + quarter, frame) * ok).astype(bf16)
    place = (pad + lane((1, fs), 1)).astype(f32)
    block = half // 4

    def inverse(i, carry):
        spot = i * block + lane((block, 1), 0)
        freq = jnp.where(spot > half, spot - half, spot).astype(f32)
        shift = jnp.where(spot > half, -quarter, 0).astype(f32)
        inv_ref[pl.ds(i * block, block)] = cos_turn(freq * place + shift, frame).astype(bf16)
        return carry

    lax.fori_loop(0, 8, inverse, 0)
    source = lax.rem(half - lane((1, half), 1), half)
    flip_ref[...] = jnp.where(lane((half, half), 0) == source, 1.0, 0.0).astype(bf16)


def column_phases_kernel(frame, fs, pos_ref, col_ref, cos_ref, sin_ref):
    ntile, ts = pos_ref.shape[1], col_ref.shape[1]
    half, quarter, pad = frame // 2, frame // 4, (frame - fs) // 2
    b_me = lax.rem(lax.axis_index("facet"), FCOLS)
    spot = lane((1, 2 * half), 1)
    freq = jnp.where(spot > half, spot - half, spot).astype(f32)
    shift = jnp.where(spot > half, quarter, 0).astype(f32)
    grain = lane((ts, 1), 0).astype(f32) * freq
    cos_ref[...] = cos_turn(grain, frame)
    sin_ref[...] = cos_turn(grain - quarter, frame)

    def columns(i, carry):
        b, t = lax.div(i, ntile), lax.rem(i, ntile)
        ox = pos_ref[1, t] - jnp.bitwise_xor(b_me, b) * fs + pad
        ok = jnp.where((ox >= 0) & (ox <= frame - ts), 1.0, 0.0).astype(f32)
        index = ox.astype(f32) * freq + shift
        cos_ox, sin_ox = cos_turn(index, frame) * ok, cos_turn(index - quarter, frame) * ok
        col_ref[i] = (cos_ox * cos_ref[...] - sin_ox * sin_ref[...]).astype(bf16)
        return carry

    lax.fori_loop(0, FCOLS * ntile, columns, 0)


def pixel_phases_kernel(frame, pad, nf, kb, count, extra, out_ref, cos_ref, sin_ref):
    me = lax.axis_index("facet")
    width = out_ref.shape[1]
    column = lane((1, width), 1)
    inner, base = column, jnp.zeros((1, width), i32)
    for j in range(nf):
        for start, rows, skip in ((j * 2 * count, 2 * count, 0), (nf * 2 * count + j * extra, extra, 2 * count)):
            here = (column >= start) & (column < start + rows)
            inner = jnp.where(here, column - start + skip, inner)
            base = jnp.where(here, jnp.bitwise_xor(me, j) * kb, base)
    k = jnp.where(inner < count, inner, inner - count)
    k = jnp.where(inner < 2 * count, k, count)
    minus_sin = ((inner >= count) & (inner < 2 * count)) | (inner == 2 * count + 1)
    shift = jnp.where(minus_sin, frame // 4, 0).astype(f32)
    k = (base + k).astype(f32)
    block = 64
    grain = lane((block, 1), 0).astype(f32) * k
    cos_ref[...] = cos_turn(grain, frame)
    sin_ref[...] = cos_turn(grain - frame // 4, frame)

    def some(i, carry):
        coarse = (pad + i * block).astype(f32) * k + shift
        cos_i, sin_i = cos_turn(coarse, frame), cos_turn(coarse - frame // 4, frame)
        out_ref[pl.ds(i * block, block)] = (cos_i * cos_ref[...] - sin_i * sin_ref[...]).astype(bf16)
        return carry

    lax.fori_loop(0, out_ref.shape[0] // block, some, 0)


def rows_kernel(total, nch, chan0, paired, psf_of_ref, coef_ref, row_ref, col_ref, inv_ref, flip_ref, psf_ref, *rest):
    far_ref, rest = (rest[0], rest[1:]) if paired else (None, rest)
    out_refs, (lhs_ref, psf_up_ref, psf_dn_ref, q_ref) = rest[:-4], rest[-4:]
    na, ntile, _, ts = row_ref.shape
    nf = coef_ref.shape[0]
    npsf, kb, frame = psf_ref.shape[0], psf_ref.shape[3], psf_ref.shape[4]
    rb = lhs_ref.shape[0] // (2 * na)
    half = frame // 2
    step = pl.program_id(1)
    first = lane((1, half), 1) == 0

    def turned(x):
        return jnp.dot(x[:, half:], flip_ref[...], preferred_element_type=f32)

    @pl.when(step == 0)
    def _():
        x = frequency(lax.axis_index("freq") * nch + chan0 + pl.program_id(0), total)
        for t in range(ntile):
            a0, a1, a2 = (
                jnp.concatenate([coef_ref[f, j * ntile + t].astype(f32) for f in range(nf)], axis=0)
                for j in range(3)
            )
            model = (a0 + a1 * x + a2 * (x * x)).astype(bf16)
            table = row_ref[:, t].reshape(na * 2 * kb, ts)
            y = jnp.dot(table, model, preferred_element_type=f32).astype(bf16)
            for part in range(2 * na):
                lhs_ref[part * rb : (part + 1) * rb, t * ts : (t + 1) * ts] = y[part * kb : part * kb + rb]
        if paired:
            count = kb // 2
            i, m = lane((rb, count), 0), lane((rb, count), 1)
            mirror = jnp.where((i >= 1) & (i < count) & (m == count - i), 1.0, 0.0).astype(bf16)
        parts = 2 * npsf
        psf = psf_ref[:, 0, :, :rb].reshape(parts * rb, frame)
        up, dn = psf[:, :half], turned(psf)
        if paired:
            far = [
                jnp.dot(mirror, far_ref[i // 2, 0, i % 2], preferred_element_type=f32).astype(bf16)
                for i in range(parts)
            ]
            far = jnp.concatenate(far, axis=0)
            far_up, far_dn = far[:, :half].astype(f32), turned(far)
            for i in range(parts):
                rows, sign = slice(i * rb, (i + 1) * rb), 1.0 - 2.0 * (i % 2)
                psf_up_ref[i // 2, i % 2] = up[rows].astype(f32) + sign * jnp.where(first, far_up[rows], far_dn[rows])
                psf_dn_ref[i // 2, i % 2] = dn[rows] + sign * jnp.where(first, far_dn[rows], far_up[rows])
        else:
            psf_up_ref[...] = up.reshape(psf_up_ref.shape)
            psf_dn_ref[...] = dn.astype(bf16).reshape(psf_dn_ref.shape)

    both = jnp.dot(lhs_ref[...], col_ref[step], preferred_element_type=f32)
    me = lax.axis_index("facet")
    zero = jnp.zeros((rb, half), f32)
    for a in range(na):
        psf = psf_of_ref[jnp.bitwise_xor(me, a * FCOLS + step)]
        top = slice(a * 2 * rb, a * 2 * rb + rb)
        low = slice(a * 2 * rb + rb, (a + 1) * 2 * rb)
        rc, rs = both[top, :half], both[top, half:]
        ic, is_ = both[low, :half], both[low, half:]
        rs0, is0 = jnp.where(first, zero, rs), jnp.where(first, zero, is_)
        up_re, up_im = rc - is0, ic + rs0
        dn_re, dn_im = jnp.where(first, rs, rc + is_), jnp.where(first, is_, ic - rs)
        p_re, p_im = psf_up_ref[psf, 0].astype(f32), psf_up_ref[psf, 1].astype(f32)
        n_re, n_im = psf_dn_ref[psf, 0].astype(f32), psf_dn_ref[psf, 1].astype(f32)
        q_re, q_im = up_re * p_re - up_im * p_im, up_re * p_im + up_im * p_re
        z_re, z_im = dn_re * n_re - dn_im * n_im, dn_re * n_im + dn_im * n_re
        q_ref[top, :half] = (q_re + jnp.where(first, zero, z_re)).astype(bf16)
        q_ref[top, half:] = jnp.where(first, z_re, z_im - q_im).astype(bf16)
        q_ref[low, :half] = (q_im + jnp.where(first, zero, z_im)).astype(bf16)
        q_ref[low, half:] = jnp.where(first, z_im, q_re - z_re).astype(bf16)
    w = jnp.dot(q_ref[...], inv_ref[...], preferred_element_type=f32)
    for b in range(FCOLS):

        @pl.when(step == b)
        def _():
            for a in range(na):
                out_ref, start = out_refs[a * FCOLS + b], a * 2 * rb
                if paired:
                    count = kb // 2
                    out_ref[0, :count] = w[start : start + count].astype(bf16)
                    out_ref[0, count : 2 * count] = w[start + rb : start + rb + count].astype(bf16)
                    re, im = start + count, start + rb + count
                    tile = (EXTRA, w.shape[1])
                    spot = lane(tile, 0)
                    extra = jnp.where(spot == 1, jnp.broadcast_to(w[im : im + 1], tile), 0.0)
                    extra = jnp.where(spot == 0, jnp.broadcast_to(w[re : re + 1], tile), extra)
                    out_ref[0, 2 * count :] = extra.astype(bf16)
                else:
                    out_ref[0] = w[start : start + 2 * rb].astype(bf16)


def pixels_kernel(nf, scale, extra, *refs):
    blocks, table_ref, residual_ref, out_ref = refs[:nf], refs[nf], refs[nf + 1], refs[-1]
    rows = blocks[0].shape[1] - extra
    w = jnp.concatenate([block[0, :rows] for block in blocks], axis=0)
    if extra:
        more = jnp.concatenate([block[0, rows:].astype(f32) for block in blocks], axis=0)
        w = jnp.concatenate([w, more.astype(bf16)], axis=0)
    conv = jnp.dot(table_ref[...], w, preferred_element_type=f32)
    out_ref[0, 0] = residual_ref[0, 0] - conv * scale


def chunks_of(nch, npair):
    sizes, left = [], nch - npair
    while left:
        sizes.append(2 if len(sizes) >= 2 and left >= 2 else 1)
        left -= sizes[-1]
    paired = [False] * len(sizes)
    while npair:
        sizes.append(1)
        npair -= sizes[-1]
        paired.append(True)
    return [(sum(sizes[:i]), n, paired[i]) for i, n in enumerate(sizes)]


def pairs_of(nch, nf, kb, frame):
    return NPAIR if nch >= NPAIR + 4 and frame == nf * kb and kb % (2 * TILE) == 0 else 0


def send_order(nf):
    return sorted(range(1, nf), key=lambda j: (-bin(j >> 1).count("1"), j))


NPAIR = 2
TILE = 16
EXTRA = 8


VMEM = pl.BlockSpec(memory_space=pltpu.VMEM)
SMEM = pl.BlockSpec(memory_space=pltpu.SMEM)


def in_hbm(x):
    return pltpu.with_memory_space_constraint(x, pltpu.HBM)


def shards(nf, nz, residual, components, chan_weight, tile_pos, facet_psf, psf_spectra):
    whole_psf = psf_spectra
    residual, psf_spectra = in_hbm(residual), in_hbm(psf_spectra)
    ntile, nch, rows, ts = components.shape
    npsf, _, _, kb, frame = psf_spectra.shape
    fs = residual.shape[2]
    pad, half = (frame - fs) // 2, frame // 2
    total = nch * nz
    na = nf // FCOLS
    npair = pairs_of(nch, nf, kb, frame)

    far = {}
    for i in range(npair):
        chan = nch - npair + i
        mirror = [(s, nf - 1 - s) for s in range(nf)]
        far[chan] = lax.ppermute(whole_psf[:, chan : chan + 1, :, kb // 2 :], "facet", mirror)
    sums = pl.pallas_call(
        functools.partial(moments_kernel, total),
        out_shape=jax.ShapeDtypeStruct((3 * ntile + 1, rows, ts), f32),
        in_specs=[SMEM, VMEM],
        out_specs=VMEM,
        compiler_params=pltpu.CompilerParams(vmem_limit_bytes=SMALL_LIMIT),
        name="moments",
    )(in_hbm(chan_weight), in_hbm(components))
    row_table, inv_table, flip = pl.pallas_call(
        functools.partial(row_phases_kernel, frame, fs),
        out_shape=[
            jax.ShapeDtypeStruct((na, ntile, 2 * kb, ts), bf16),
            pltpu.HBM((frame, fs), bf16),
            pltpu.HBM((half, half), bf16),
        ],
        grid=(1,),
        in_specs=[SMEM],
        out_specs=[
            VMEM,
            pl.BlockSpec((frame, fs), lambda i: (0, 0)),
            pl.BlockSpec((half, half), lambda i: (0, 0)),
        ],
        compiler_params=pltpu.CompilerParams(vmem_limit_bytes=SMALL_LIMIT),
        name="rowphases",
    )(in_hbm(tile_pos.T))
    col_table = pl.pallas_call(
        functools.partial(column_phases_kernel, frame, fs),
        out_shape=jax.ShapeDtypeStruct((FCOLS * ntile, ts, frame), bf16),
        in_specs=[SMEM],
        out_specs=VMEM,
        scratch_shapes=[pltpu.VMEM((ts, frame), f32)] * 2,
        compiler_params=pltpu.CompilerParams(vmem_limit_bytes=SMALL_LIMIT),
        name="colphases",
    )(in_hbm(tile_pos.T))
    col_table = col_table.reshape(FCOLS, ntile * ts, frame)
    other = jnp.zeros_like(sums)
    for i in range(nz.bit_length() - 1):
        if i:
            sums = sums + other
        other = lax.ppermute(sums, "freq", [(s, s ^ (1 << i)) for s in range(nz)])
    fit = pl.pallas_call(
        solve_kernel,
        out_shape=jax.ShapeDtypeStruct((3 * ntile + 1, rows, ts), bf16),
        in_specs=[SMEM, VMEM, VMEM],
        out_specs=VMEM,
        compiler_params=pltpu.CompilerParams(vmem_limit_bytes=SMALL_LIMIT),
        name="solve",
    )(facet_psf, sums, other)
    fit = lax.all_gather(fit, "facet", axis=0)
    psf_of = fit[:, 3 * ntile, 0, 0].astype(i32)
    rb_pair, block_pair = kb // 2 + TILE, kb + EXTRA
    tables = {}
    for paired in (False, True)[: 1 + bool(npair)]:
        tables[paired] = pl.pallas_call(
            functools.partial(
                pixel_phases_kernel, frame, pad, nf, kb, kb // 2 if paired else kb, EXTRA * paired
            ),
            out_shape=jax.ShapeDtypeStruct((fs, nf * (block_pair if paired else 2 * kb)), bf16),
            out_specs=VMEM,
            scratch_shapes=[pltpu.VMEM((64, nf * (block_pair if paired else 2 * kb)), f32)] * 2,
            compiler_params=pltpu.CompilerParams(vmem_limit_bytes=VMEM_LIMIT),
            name="pixphases",
        )()

    pieces = []
    for chan0, count, paired in chunks_of(nch, npair):
        rb, block = (rb_pair, block_pair) if paired else (kb, 2 * kb)
        psf_type = f32 if paired else bf16
        w = pl.pallas_call(
            functools.partial(rows_kernel, total, nch, chan0, paired),
            grid_spec=pltpu.PrefetchScalarGridSpec(
                num_scalar_prefetch=1,
                grid=(count, FCOLS),
                in_specs=[
                    VMEM,
                    VMEM,
                    VMEM,
                    pl.BlockSpec((frame, fs), lambda c, b, s: (0, 0)),
                    pl.BlockSpec((half, half), lambda c, b, s: (0, 0)),
                    pl.BlockSpec((npsf, 1, 2, kb, frame), lambda c, b, s, c0=chan0: (0, c0 + c, 0, 0, 0)),
                ]
                + [
                    pl.BlockSpec(
                        (npsf, 1, 2, kb // 2, frame),
                        lambda c, b, s: (0, c, 0, 0, 0),
                    )
                ]
                * paired,
                out_specs=[pl.BlockSpec((1, block, fs), lambda c, b, s: (c, 0, 0))] * nf,
                scratch_shapes=[
                    pltpu.VMEM((na * 2 * rb, ntile * ts), bf16),
                    pltpu.VMEM((npsf, 2, rb, half), psf_type),
                    pltpu.VMEM((npsf, 2, rb, half), psf_type),
                    pltpu.VMEM((na * 2 * rb, frame), bf16),
                ],
            ),
            out_shape=[pltpu.HBM((count, block, fs), bf16)] * nf,
            cost_estimate=pl.CostEstimate(
                flops=count * nf * 4 * rb * frame * (ntile * ts + fs),
                bytes_accessed=count * (npsf * 4 * kb * frame + nf * 2 * block * fs) + 8 * ntile * ts * frame,
                transcendentals=0,
            ),
            compiler_params=pltpu.CompilerParams(vmem_limit_bytes=VMEM_LIMIT),
            name="rows",
        )(psf_of, fit, row_table, col_table, in_hbm(inv_table), in_hbm(flip), psf_spectra, *([far[chan0]] if paired else []))
        got = list(w)
        for j in send_order(nf):
            got[j] = lax.ppermute(w[j], "facet", [(s, s ^ j) for s in range(nf)])
        pieces.append((chan0, count, block, tables[paired], got))
    result = None
    for chan0, count, block, pix_table, got in pieces:
        image = pl.BlockSpec((1, 1, fs, fs), lambda c, c0=chan0: (c0 + c, 0, 0, 0))
        before = [] if result is None else [result]
        result = pl.pallas_call(
            functools.partial(
                pixels_kernel, nf, 1.0 / (frame * frame), EXTRA if block == block_pair else 0
            ),
            grid=(count,),
            in_specs=[pl.BlockSpec((1, block, fs), lambda c: (c, 0, 0))] * nf
            + [VMEM, image]
            + [pl.BlockSpec(memory_space=pl.ANY)] * len(before),
            out_specs=image,
            out_shape=jax.ShapeDtypeStruct(residual.shape, f32),
            input_output_aliases={nf + 2: 0} if before else {},
            cost_estimate=pl.CostEstimate(
                flops=count * 2 * fs * nf * block * fs,
                bytes_accessed=count * (nf * 2 * block * fs + 8 * fs * fs),
                transcendentals=0,
            ),
            compiler_params=pltpu.CompilerParams(vmem_limit_bytes=VMEM_LIMIT),
            name="pixels",
        )(*got, pix_table, residual, *before)
    return result


def solution(mesh):
    placed = (
        P("freq", "facet", None, None),
        P(None, "freq", "facet", None),
        P("freq"),
        P(),
        P("facet"),
        P(None, "freq", None, "facet", None),
    )
    nf, nz = mesh.shape["facet"], mesh.shape["freq"]

    def step(*args):
        return shards(nf, nz, *args)

    return jax.shard_map(
        step,
        mesh=mesh,
        in_specs=placed,
        out_specs=P("freq", "facet", None, None),
        check_vma=False,
    )
```

```python
import functools
import math

import jax
import jax.numpy as jnp
from jax import lax
from jax.experimental import pallas as pl
from jax.experimental.pallas import tpu as pltpu
from jax.sharding import PartitionSpec as P

FCOLS = 4
VMEM_LIMIT = 20 * 1024 * 1024
SMALL_LIMIT = 10 * 1024 * 1024

bf16, f32, i32 = jnp.bfloat16, jnp.float32, jnp.int32


def frequency(chan, total):
    return (2.0 * chan.astype(f32) - (total - 1)) * (1.0 / total)


def moments_kernel(total, weight_ref, comp_ref, out_ref):
    ntile, nch = comp_ref.shape[:2]
    first = lax.axis_index("freq") * nch
    power = [[], [], []]
    gram = [jnp.float32(0.0)] * 5
    for c in range(nch):
        x = frequency(first + c, total)
        w = weight_ref[c]
        terms = (w, w * x, w * x * x)
        for j in range(3):
            power[j].append(terms[j])
            gram[j] = gram[j] + terms[j]
        gram[3] = gram[3] + terms[2] * x
        gram[4] = gram[4] + terms[2] * x * x
    for t in range(ntile):
        acc = [None] * 3
        for c in range(nch):
            comp = comp_ref[t, c].astype(f32)
            for j in range(3):
                term = power[j][c] * comp
                acc[j] = term if c == 0 else acc[j] + term
        for j in range(3):
            out_ref[j * ntile + t] = acc[j]
    for j in range(5):
        out_ref[3 * ntile, j : j + 1] = jnp.full((1, out_ref.shape[2]), gram[j], f32)
    rest = out_ref.shape[1] - 5
    out_ref[3 * ntile, 5:] = jnp.zeros((rest, out_ref.shape[2]), f32)


def solve_kernel(psf_ref, one_ref, two_ref, out_ref):
    ntile = (out_ref.shape[0] - 1) // 3
    gram = one_ref[3 * ntile] + two_ref[3 * ntile]
    g0, g1, g2, g3, g4 = (gram[j : j + 1] for j in range(5))
    c00 = g2 * g4 - g3 * g3
    c01 = g2 * g3 - g1 * g4
    c02 = g1 * g3 - g2 * g2
    c11 = g0 * g4 - g2 * g2
    c12 = g1 * g2 - g0 * g3
    c22 = g0 * g2 - g1 * g1
    det = g0 * c00 + g1 * c01 + g2 * c02
    for t in range(ntile):
        m0, m1, m2 = (one_ref[j * ntile + t] + two_ref[j * ntile + t] for j in range(3))
        out_ref[t] = ((c00 * m0 + c01 * m1 + c02 * m2) / det).astype(bf16)
        out_ref[ntile + t] = ((c01 * m0 + c11 * m1 + c12 * m2) / det).astype(bf16)
        out_ref[2 * ntile + t] = ((c02 * m0 + c12 * m1 + c22 * m2) / det).astype(bf16)
    out_ref[3 * ntile] = jnp.full(out_ref.shape[1:], psf_ref[0].astype(f32), f32).astype(bf16)


def cos_turn(index, frame):
    rest = jnp.abs(index - frame * jnp.floor(index * (1.0 / frame) + 0.5))
    x = (frame // 4 - rest) * (2.0 * math.pi / frame)
    square = x * x
    poly = jnp.full_like(square, 1.0 / math.factorial(13))
    for n in (11, 9, 7, 5, 3, 1):
        poly = poly * square + (-1.0) ** ((n - 1) // 2) / math.factorial(n)
    return poly * x


def lane(shape, axis):
    return lax.broadcasted_iota(i32, shape, axis)


def inverse_phases_kernel(frame, fs, inv_ref):
    half, quarter, pad = frame // 2, frame // 4, (frame - fs) // 2
    place = (pad + lane((1, fs), 1)).astype(f32)
    block = half // 4

    def inverse(i, carry):
        spot = i * block + lane((block, 1), 0)
        freq = jnp.where(spot > half, spot - half, spot).astype(f32)
        shift = jnp.where(spot > half, -quarter, 0).astype(f32)
        inv_ref[pl.ds(i * block, block)] = cos_turn(freq * place + shift, frame).astype(bf16)
        return carry

    lax.fori_loop(0, 8, inverse, 0)


def row_phases_kernel(frame, fs, pos_ref, row_ref, flip_ref):
    na, ntile, two_kb, ts = row_ref.shape
    kb = two_kb // 2
    half, quarter, pad = frame // 2, frame // 4, (frame - fs) // 2
    me = lax.axis_index("facet")
    a_me = lax.div(me, FCOLS)
    pixel = lane((1, ts), 1)
    own = (me * kb + lane((kb, 1), 0)).astype(f32)
    for a in range(na):
        for t in range(ntile):
            oy = pos_ref[0, t] - jnp.bitwise_xor(a_me, a) * fs + pad
            ok = jnp.where((oy >= 0) & (oy <= frame - ts), 1.0, 0.0).astype(f32)
            index = own * (oy + pixel).astype(f32)
            row_ref[a, t, :kb] = (cos_turn(index, frame) * ok).astype(bf16)
            row_ref[a, t, kb:] = (cos_turn(index + quarter, frame) * ok).astype(bf16)
    source = lax.rem(half - lane((1, half), 1), half)
    flip_ref[...] = jnp.where(lane((half, half), 0) == source, 1.0, 0.0).astype(bf16)


def column_phases_kernel(frame, fs, pos_ref, col_ref, cos_ref, sin_ref):
    ntile, ts = pos_ref.shape[1], col_ref.shape[1]
    half, quarter, pad = frame // 2, frame // 4, (frame - fs) // 2
    b_me = lax.rem(lax.axis_index("facet"), FCOLS)
    spot = lane((1, 2 * half), 1)
    freq = jnp.where(spot > half, spot - half, spot).astype(f32)
    shift = jnp.where(spot > half, quarter, 0).astype(f32)
    grain = lane((ts, 1), 0).astype(f32) * freq
    cos_ref[...] = cos_turn(grain, frame)
    sin_ref[...] = cos_turn(grain - quarter, frame)

    def columns(i, carry):
        b, t = lax.div(i, ntile), lax.rem(i, ntile)
        ox = pos_ref[1, t] - jnp.bitwise_xor(b_me, b) * fs + pad
        ok = jnp.where((ox >= 0) & (ox <= frame - ts), 1.0, 0.0).astype(f32)
        index = ox.astype(f32) * freq + shift
        cos_ox, sin_ox = cos_turn(index, frame) * ok, cos_turn(index - quarter, frame) * ok
        col_ref[i] = (cos_ox * cos_ref[...] - sin_ox * sin_ref[...]).astype(bf16)
        return carry

    lax.fori_loop(0, FCOLS * ntile, columns, 0)


def pixel_phases_kernel(frame, pad, nf, kb, count, extra, out_ref, cos_ref, sin_ref):
    me = lax.axis_index("facet")
    width = out_ref.shape[1]
    column = lane((1, width), 1)
    inner, base = column, jnp.zeros((1, width), i32)
    for j in range(nf):
        for start, rows, skip in ((j * 2 * count, 2 * count, 0), (nf * 2 * count + j * extra, extra, 2 * count)):
            here = (column >= start) & (column < start + rows)
            inner = jnp.where(here, column - start + skip, inner)
            base = jnp.where(here, jnp.bitwise_xor(me, j) * kb, base)
    k = jnp.where(inner < count, inner, inner - count)
    k = jnp.where(inner < 2 * count, k, count)
    minus_sin = ((inner >= count) & (inner < 2 * count)) | (inner == 2 * count + 1)
    shift = jnp.where(minus_sin, frame // 4, 0).astype(f32)
    k = (base + k).astype(f32)
    block = 64
    grain = lane((block, 1), 0).astype(f32) * k
    cos_ref[...] = cos_turn(grain, frame)
    sin_ref[...] = cos_turn(grain - frame // 4, frame)

    def some(i, carry):
        coarse = (pad + i * block).astype(f32) * k + shift
        cos_i, sin_i = cos_turn(coarse, frame), cos_turn(coarse - frame // 4, frame)
        out_ref[pl.ds(i * block, block)] = (cos_i * cos_ref[...] - sin_i * sin_ref[...]).astype(bf16)
        return carry

    lax.fori_loop(0, out_ref.shape[0] // block, some, 0)


def rows_kernel(total, nch, chan0, paired, psf_of_ref, coef_ref, row_ref, col_ref, inv_ref, flip_ref, psf_ref, *rest):
    far_ref, rest = (rest[0], rest[1:]) if paired else (None, rest)
    out_refs, (lhs_ref, psf_up_ref, psf_dn_ref, q_ref) = rest[:-4], rest[-4:]
    na, ntile, _, ts = row_ref.shape
    nf = coef_ref.shape[0]
    npsf, kb, frame = psf_ref.shape[0], psf_ref.shape[3], psf_ref.shape[4]
    rb = lhs_ref.shape[0] // (2 * na)
    half = frame // 2
    step = pl.program_id(1)
    first = lane((1, half), 1) == 0

    def turned(x):
        return jnp.dot(x[:, half:], flip_ref[...], preferred_element_type=f32)

    @pl.when(step == 0)
    def _():
        x = frequency(lax.axis_index("freq") * nch + chan0 + pl.program_id(0), total)
        for t in range(ntile):
            a0, a1, a2 = (
                jnp.concatenate([coef_ref[f, j * ntile + t].astype(f32) for f in range(nf)], axis=0)
                for j in range(3)
            )
            model = (a0 + a1 * x + a2 * (x * x)).astype(bf16)
            table = row_ref[:, t].reshape(na * 2 * kb, ts)
            y = jnp.dot(table, model, preferred_element_type=f32).astype(bf16)
            for part in range(2 * na):
                lhs_ref[part * rb : (part + 1) * rb, t * ts : (t + 1) * ts] = y[part * kb : part * kb + rb]
        if paired:
            count = kb // 2
            i, m = lane((rb, count), 0), lane((rb, count), 1)
            mirror = jnp.where((i >= 1) & (i < count) & (m == count - i), 1.0, 0.0).astype(bf16)
        parts = 2 * npsf
        psf = psf_ref[:, 0, :, :rb].reshape(parts * rb, frame)
        up, dn = psf[:, :half], turned(psf)
        if paired:
            far = [
                jnp.dot(mirror, far_ref[i // 2, 0, i % 2], preferred_element_type=f32).astype(bf16)
                for i in range(parts)
            ]
            far = jnp.concatenate(far, axis=0)
            far_up, far_dn = far[:, :half].astype(f32), turned(far)
            for i in range(parts):
                rows, sign = slice(i * rb, (i + 1) * rb), 1.0 - 2.0 * (i % 2)
                psf_up_ref[i // 2, i % 2] = up[rows].astype(f32) + sign * jnp.where(first, far_up[rows], far_dn[rows])
                psf_dn_ref[i // 2, i % 2] = dn[rows] + sign * jnp.where(first, far_dn[rows], far_up[rows])
        else:
            psf_up_ref[...] = up.reshape(psf_up_ref.shape)
            psf_dn_ref[...] = dn.astype(bf16).reshape(psf_dn_ref.shape)

    both = jnp.dot(lhs_ref[...], col_ref[step], preferred_element_type=f32)
    me = lax.axis_index("facet")
    zero = jnp.zeros((rb, half), f32)
    for a in range(na):
        psf = psf_of_ref[jnp.bitwise_xor(me, a * FCOLS + step)]
        top = slice(a * 2 * rb, a * 2 * rb + rb)
        low = slice(a * 2 * rb + rb, (a + 1) * 2 * rb)
        rc, rs = both[top, :half], both[top, half:]
        ic, is_ = both[low, :half], both[low, half:]
        rs0, is0 = jnp.where(first, zero, rs), jnp.where(first, zero, is_)
        up_re, up_im = rc - is0, ic + rs0
        dn_re, dn_im = jnp.where(first, rs, rc + is_), jnp.where(first, is_, ic - rs)
        p_re, p_im = psf_up_ref[psf, 0].astype(f32), psf_up_ref[psf, 1].astype(f32)
        n_re, n_im = psf_dn_ref[psf, 0].astype(f32), psf_dn_ref[psf, 1].astype(f32)
        q_re, q_im = up_re * p_re - up_im * p_im, up_re * p_im + up_im * p_re
        z_re, z_im = dn_re * n_re - dn_im * n_im, dn_re * n_im + dn_im * n_re
        q_ref[top, :half] = (q_re + jnp.where(first, zero, z_re)).astype(bf16)
        q_ref[top, half:] = jnp.where(first, z_re, z_im - q_im).astype(bf16)
        q_ref[low, :half] = (q_im + jnp.where(first, zero, z_im)).astype(bf16)
        q_ref[low, half:] = jnp.where(first, z_im, q_re - z_re).astype(bf16)
    w = jnp.dot(q_ref[...], inv_ref[...], preferred_element_type=f32)
    for b in range(FCOLS):

        @pl.when(step == b)
        def _():
            for a in range(na):
                out_ref, start = out_refs[a * FCOLS + b], a * 2 * rb
                if paired:
                    count = kb // 2
                    out_ref[0, :count] = w[start : start + count].astype(bf16)
                    out_ref[0, count : 2 * count] = w[start + rb : start + rb + count].astype(bf16)
                    re, im = start + count, start + rb + count
                    tile = (EXTRA, w.shape[1])
                    spot = lane(tile, 0)
                    extra = jnp.where(spot == 1, jnp.broadcast_to(w[im : im + 1], tile), 0.0)
                    extra = jnp.where(spot == 0, jnp.broadcast_to(w[re : re + 1], tile), extra)
                    out_ref[0, 2 * count :] = extra.astype(bf16)
                else:
                    out_ref[0] = w[start : start + 2 * rb].astype(bf16)


def pixels_kernel(nf, scale, extra, *refs):
    blocks, table_ref, residual_ref, out_ref = refs[:nf], refs[nf], refs[nf + 1], refs[-1]
    rows = blocks[0].shape[1] - extra
    w = jnp.concatenate([block[0, :rows] for block in blocks], axis=0)
    if extra:
        more = jnp.concatenate([block[0, rows:].astype(f32) for block in blocks], axis=0)
        w = jnp.concatenate([w, more.astype(bf16)], axis=0)
    conv = jnp.dot(table_ref[...], w, preferred_element_type=f32)
    out_ref[0, 0] = residual_ref[0, 0] - conv * scale


def chunks_of(nch, npair):
    sizes, left = [], nch - npair
    while left:
        sizes.append(2 if len(sizes) >= 2 and left >= 2 else 1)
        left -= sizes[-1]
    paired = [False] * len(sizes)
    while npair:
        sizes.append(1)
        npair -= sizes[-1]
        paired.append(True)
    return [(sum(sizes[:i]), n, paired[i]) for i, n in enumerate(sizes)]


def pairs_of(nch, nf, kb, frame):
    return NPAIR if nch >= NPAIR + 4 and frame == nf * kb and kb % (2 * TILE) == 0 else 0


def send_order(nf):
    return sorted(range(1, nf), key=lambda j: (-bin(j >> 1).count("1"), j))


NPAIR = 2
TILE = 16
EXTRA = 8


VMEM = pl.BlockSpec(memory_space=pltpu.VMEM)
SMEM = pl.BlockSpec(memory_space=pltpu.SMEM)


def in_hbm(x):
    return pltpu.with_memory_space_constraint(x, pltpu.HBM)


def shards(nf, nz, residual, components, chan_weight, tile_pos, facet_psf, psf_spectra):
    whole_psf = psf_spectra
    residual, psf_spectra = in_hbm(residual), in_hbm(psf_spectra)
    ntile, nch, rows, ts = components.shape
    npsf, _, _, kb, frame = psf_spectra.shape
    fs = residual.shape[2]
    pad, half = (frame - fs) // 2, frame // 2
    total = nch * nz
    na = nf // FCOLS
    npair = pairs_of(nch, nf, kb, frame)

    far = {}
    for i in range(npair):
        chan = nch - npair + i
        mirror = [(s, nf - 1 - s) for s in range(nf)]
        far[chan] = lax.ppermute(whole_psf[:, chan : chan + 1, :, kb // 2 :], "facet", mirror)
    sums = pl.pallas_call(
        functools.partial(moments_kernel, total),
        out_shape=jax.ShapeDtypeStruct((3 * ntile + 1, rows, ts), f32),
        in_specs=[SMEM, VMEM],
        out_specs=VMEM,
        compiler_params=pltpu.CompilerParams(vmem_limit_bytes=SMALL_LIMIT),
        name="moments",
    )(in_hbm(chan_weight), in_hbm(components))
    row_table, flip = pl.pallas_call(
        functools.partial(row_phases_kernel, frame, fs),
        out_shape=[
            jax.ShapeDtypeStruct((na, ntile, 2 * kb, ts), bf16),
            pltpu.HBM((half, half), bf16),
        ],
        grid=(1,),
        in_specs=[SMEM],
        out_specs=[
            VMEM,
            pl.BlockSpec((half, half), lambda i: (0, 0)),
        ],
        compiler_params=pltpu.CompilerParams(vmem_limit_bytes=SMALL_LIMIT),
        name="rowphases",
    )(in_hbm(tile_pos.T))
    inv_table = pl.pallas_call(
        functools.partial(inverse_phases_kernel, frame, fs),
        out_shape=pltpu.HBM((frame, fs), bf16),
        grid=(1,),
        out_specs=pl.BlockSpec((frame, fs), lambda i: (0, 0)),
        compiler_params=pltpu.CompilerParams(vmem_limit_bytes=SMALL_LIMIT),
        name="invphases",
    )()
    col_table = pl.pallas_call(
        functools.partial(column_phases_kernel, frame, fs),
        out_shape=jax.ShapeDtypeStruct((FCOLS * ntile, ts, frame), bf16),
        in_specs=[SMEM],
        out_specs=VMEM,
        scratch_shapes=[pltpu.VMEM((ts, frame), f32)] * 2,
        compiler_params=pltpu.CompilerParams(vmem_limit_bytes=SMALL_LIMIT),
        name="colphases",
    )(in_hbm(tile_pos.T))
    col_table = col_table.reshape(FCOLS, ntile * ts, frame)
    other = jnp.zeros_like(sums)
    for i in range(nz.bit_length() - 1):
        if i:
            sums = sums + other
        other = lax.ppermute(sums, "freq", [(s, s ^ (1 << i)) for s in range(nz)])
    fit = pl.pallas_call(
        solve_kernel,
        out_shape=jax.ShapeDtypeStruct((3 * ntile + 1, rows, ts), bf16),
        in_specs=[SMEM, VMEM, VMEM],
        out_specs=VMEM,
        compiler_params=pltpu.CompilerParams(vmem_limit_bytes=SMALL_LIMIT),
        name="solve",
    )(facet_psf, sums, other)
    fit = lax.all_gather(fit, "facet", axis=0)
    psf_of = fit[:, 3 * ntile, 0, 0].astype(i32)
    rb_pair, block_pair = kb // 2 + TILE, kb + EXTRA
    tables = {}
    for paired in (False, True)[: 1 + bool(npair)]:
        tables[paired] = pl.pallas_call(
            functools.partial(
                pixel_phases_kernel, frame, pad, nf, kb, kb // 2 if paired else kb, EXTRA * paired
            ),
            out_shape=jax.ShapeDtypeStruct((fs, nf * (block_pair if paired else 2 * kb)), bf16),
            out_specs=VMEM,
            scratch_shapes=[pltpu.VMEM((64, nf * (block_pair if paired else 2 * kb)), f32)] * 2,
            compiler_params=pltpu.CompilerParams(vmem_limit_bytes=VMEM_LIMIT),
            name="pixphases",
        )()

    pieces = []
    for chan0, count, paired in chunks_of(nch, npair):
        rb, block = (rb_pair, block_pair) if paired else (kb, 2 * kb)
        psf_type = f32 if paired else bf16
        w = pl.pallas_call(
            functools.partial(rows_kernel, total, nch, chan0, paired),
            grid_spec=pltpu.PrefetchScalarGridSpec(
                num_scalar_prefetch=1,
                grid=(count, FCOLS),
                in_specs=[
                    VMEM,
                    VMEM,
                    VMEM,
                    pl.BlockSpec((frame, fs), lambda c, b, s: (0, 0)),
                    pl.BlockSpec((half, half), lambda c, b, s: (0, 0)),
                    pl.BlockSpec((npsf, 1, 2, kb, frame), lambda c, b, s, c0=chan0: (0, c0 + c, 0, 0, 0)),
                ]
                + [
                    pl.BlockSpec(
                        (npsf, 1, 2, kb // 2, frame),
                        lambda c, b, s: (0, c, 0, 0, 0),
                    )
                ]
                * paired,
                out_specs=[pl.BlockSpec((1, block, fs), lambda c, b, s: (c, 0, 0))] * nf,
                scratch_shapes=[
                    pltpu.VMEM((na * 2 * rb, ntile * ts), bf16),
                    pltpu.VMEM((npsf, 2, rb, half), psf_type),
                    pltpu.VMEM((npsf, 2, rb, half), psf_type),
                    pltpu.VMEM((na * 2 * rb, frame), bf16),
                ],
            ),
            out_shape=[pltpu.HBM((count, block, fs), bf16)] * nf,
            cost_estimate=pl.CostEstimate(
                flops=count * nf * 4 * rb * frame * (ntile * ts + fs),
                bytes_accessed=count * (npsf * 4 * kb * frame + nf * 2 * block * fs) + 8 * ntile * ts * frame,
                transcendentals=0,
            ),
            compiler_params=pltpu.CompilerParams(vmem_limit_bytes=VMEM_LIMIT),
            name="rows",
        )(psf_of, fit, row_table, col_table, in_hbm(inv_table), in_hbm(flip), psf_spectra, *([far[chan0]] if paired else []))
        got = list(w)
        for j in send_order(nf):
            got[j] = lax.ppermute(w[j], "facet", [(s, s ^ j) for s in range(nf)])
        pieces.append((chan0, count, block, tables[paired], got))
    result = None
    for chan0, count, block, pix_table, got in pieces:
        image = pl.BlockSpec((1, 1, fs, fs), lambda c, c0=chan0: (c0 + c, 0, 0, 0))
        before = [] if result is None else [result]
        result = pl.pallas_call(
            functools.partial(
                pixels_kernel, nf, 1.0 / (frame * frame), EXTRA if block == block_pair else 0
            ),
            grid=(count,),
            in_specs=[pl.BlockSpec((1, block, fs), lambda c: (c, 0, 0))] * nf
            + [VMEM, image]
            + [pl.BlockSpec(memory_space=pl.ANY)] * len(before),
            out_specs=image,
            out_shape=jax.ShapeDtypeStruct(residual.shape, f32),
            input_output_aliases={nf + 2: 0} if before else {},
            cost_estimate=pl.CostEstimate(
                flops=count * 2 * fs * nf * block * fs,
                bytes_accessed=count * (nf * 2 * block * fs + 8 * fs * fs),
                transcendentals=0,
            ),
            compiler_params=pltpu.CompilerParams(vmem_limit_bytes=VMEM_LIMIT),
            name="pixels",
        )(*got, pix_table, residual, *before)
    return result


def solution(mesh):
    placed = (
        P("freq", "facet", None, None),
        P(None, "freq", "facet", None),
        P("freq"),
        P(),
        P("facet"),
        P(None, "freq", None, "facet", None),
    )
    nf, nz = mesh.shape["facet"], mesh.shape["freq"]

    def step(*args):
        return shards(nf, nz, *args)

    return jax.shard_map(
        step,
        mesh=mesh,
        in_specs=placed,
        out_specs=P("freq", "facet", None, None),
        check_vma=False,
    )
```
